32 devices in a mesh: gx: 4 (over z), gy: 8 (over y, x, core).
Axes of the slice: x: 2, y: 2, z: 4, core: 2. Of those that a mesh axis runs over, the one named last changes fastest.
Arguments:
- features: bfloat16 [4, 8, 1600, 128], P('gx', 'gy'), may hold values from -6 to 6
- cotangent: bfloat16 [4, 8, 1600, 128], P('gx', 'gy'), may hold values from -6 to 6
- w_order0: bfloat16 [320, 320], replicated, may hold values from -0.3125 to 0.3125
- w_order1: bfloat16 [2, 256, 256], replicated, may hold values from -0.375 to 0.375
- w_order2: bfloat16 [2, 192, 192], replicated, may hold values from -0.4375 to 0.4375
- w_order3: bfloat16 [2, 128, 128], replicated, may hold values from -0.5 to 0.5
- w_order4: bfloat16 [2, 64, 64], replicated, may hold values from -0.75 to 0.75
- to_grid: float32 [100, 25], replicated, may hold values from -1.25 to 1.25
- from_grid: float32 [25, 100], replicated, may hold values from -0.625 to 0.625
- edge_harmonics: float32 [4, 8, 25, 256], P('gx', 'gy'), may hold values from -5 to 5
- edge_source: int32 [4, 8, 256], P('gx', 'gy'), may hold values from 0 to 383, as said below
- edge_target: int32 [4, 8, 256], P('gx', 'gy'), may hold values from 0 to 128, as said below
- send_list: int32 [4, 8, 8, 32], P('gx', 'gy'), may hold values from 0 to 127, as said below
Outputs:
- layer_out: bfloat16 [4, 8, 1600, 128], P('gx', 'gy')
- feature_grad: float32 [4, 8, 1600, 128], P('gx', 'gy')
The draws below stay inside these ranges and needn't reach their ends.
Inputs may be any that keep to these rules, and one draw needn't show every extreme that they name: `edge_source`: on each cell the live edges come first and padding follows; the number of live edges of a cell is at least 128, and all 256 slots are live on some cell in every draw. Columns below 128 are owned atoms, column 128 + d * 32 + i is entry i of ghost block d. `edge_target`: the value 128 marks a padded edge slot, exactly those slots after a cell's live edges. `send_list`: the 32 entries of one cell and one direction are distinct.
All inputs are finite; a program needn't handle non-finite values.
Results may differ from the reference program's by a relative error of at most 0.0034.
Values may be sent and summed in bfloat16 or wider, within the bound.
No kernel may reach another device: no remote copies, remote signals or barrier semaphores. Data moves between devices by JAX's collectives and lax.ppermute only.
A program may use at most 64 MiB of HBM per device.

```python
import jax
import jax.numpy as jnp
from jax import lax

CH = 64
GRID = 100
ATOM_DEV = 128
EDGE_BLOCK = 128
EDGE_DEV = 256
GHOST = 32
N_GX = 4
N_GY = 8


def edge_layout(key):
    base = jax.random.fold_in(key, 11)
    subkeys = jax.random.split(base, 6)
    cell_count = N_GX * N_GY
    uniform_pick = jax.random.randint(subkeys[0], (cell_count,), 0, 1001)
    fraction = uniform_pick * uniform_pick * uniform_pick // 1000000
    minimum = EDGE_BLOCK
    live_edges = minimum + (EDGE_DEV - minimum) * fraction // 1000
    fullest = jax.random.randint(subkeys[1], (), 0, cell_count)
    live_edges = jnp.where(jnp.arange(cell_count) == fullest, EDGE_DEV, live_edges)
    slot_ids = jnp.arange(EDGE_DEV)[None, :]
    is_live = slot_ids < live_edges[:, None]
    shape = (cell_count, EDGE_DEV)
    targets = jax.random.randint(subkeys[2], shape, 0, ATOM_DEV)
    targets = jnp.where(is_live, targets, ATOM_DEV)
    from_ghost = jax.random.randint(subkeys[3], shape, 0, 5) < 2
    own_source = jax.random.randint(subkeys[4], shape, 0, ATOM_DEV)
    ghost_source = ATOM_DEV + jax.random.randint(subkeys[5], shape, 0, 8 * GHOST)
    sources = jnp.where(is_live, jnp.where(from_ghost, ghost_source, own_source), 0)
    return (sources.reshape(N_GX, N_GY, EDGE_DEV), targets.reshape(N_GX, N_GY, EDGE_DEV))


def draw_edge_source(key, part):
    return edge_layout(key)[0]


def draw_edge_target(key, part):
    return edge_layout(key)[1]


def draw_send_list(key, part):
    base = jax.random.fold_in(key, 23)
    subkeys = jax.random.split(base, N_GX * N_GY * 8)

    def one_list(single):
        return jax.random.permutation(single, ATOM_DEV)[:GHOST]
    lists = jax.vmap(one_list)(subkeys)
    return lists.reshape(N_GX, N_GY, 8, GHOST)


def shard_levels(stream_key, shape, cuts, low, largest):
    def one(axis_at, blocks):
        draws = jax.random.uniform(jax.random.fold_in(jax.random.fold_in(stream_key, 6), axis_at), (blocks,), jnp.float32, low / len(cuts), largest / len(cuts))
        return jnp.repeat(jnp.exp(draws), shape[axis_at] // blocks).reshape((-1,) + (1,) * (len(shape) - axis_at - 1))

    loudness = one(*cuts[0])
    for cut in cuts[1:]:
        loudness = loudness * one(*cut)
    return loudness


def gaussian(key, extent, scale, reach, shards=(), held_as=jnp.bfloat16):
    result = jax.random.normal(key, extent, jnp.float32) * scale
    if len(shards) > 0:
        result = shard_levels(key, extent, shards, -0.22, 0.18) * result
    return jnp.clip(result, min=-reach, max=reach).astype(held_as)


def setup_inputs(seed: int = 0) -> dict:
    arg_keys = jax.random.split(jax.random.key(seed), 14)
    return {
        "features": gaussian(arg_keys[0], (N_GX, N_GY, 25 * CH, ATOM_DEV), 1.0, 6.0, ((0, 4), (1, 8))),
        "cotangent": gaussian(arg_keys[1], (N_GX, N_GY, 25 * CH, ATOM_DEV), 1.0, 6.0, ((0, 4), (1, 8))),
        "w_order0": gaussian(arg_keys[2], (5 * CH, 5 * CH), (5 * CH) ** -0.5, 0.3125),
        "w_order1": gaussian(arg_keys[3], (2, 4 * CH, 4 * CH), (4 * CH) ** -0.5, 0.375),
        "w_order2": gaussian(arg_keys[4], (2, 3 * CH, 3 * CH), (3 * CH) ** -0.5, 0.4375),
        "w_order3": gaussian(arg_keys[5], (2, 2 * CH, 2 * CH), (2 * CH) ** -0.5, 0.5),
        "w_order4": gaussian(arg_keys[6], (2, CH, CH), CH ** -0.5, 0.75),
        "to_grid": gaussian(arg_keys[7], (GRID, 25), 25 ** -0.5, 1.25, (), jnp.float32),
        "from_grid": gaussian(arg_keys[8], (25, GRID), GRID ** -0.5, 0.625, (), jnp.float32),
        "edge_harmonics": gaussian(arg_keys[9], (N_GX, N_GY, 25, EDGE_DEV), 1.0, 5.0, ((0, 4), (1, 8)), jnp.float32),
        "edge_source": draw_edge_source(jax.random.fold_in(arg_keys[13], 71), 0),
        "edge_target": draw_edge_target(jax.random.fold_in(arg_keys[13], 71), 0),
        "send_list": draw_send_list(jax.random.fold_in(arg_keys[13], 71), 0),
    }


DIRECTIONS = ((-1, -1), (-1, 0), (-1, 1), (0, -1), (0, 1), (1, -1), (1, 0), (1, 1))
edge_norm = 0.35


def order_spans(channels):
    spans = []
    offset = 5 * channels
    for degree_gap in range(1, 5):
        length = (5 - degree_gap) * channels
        spans.append((offset, offset + length, offset + 2 * length))
        offset = offset + 2 * length
    return spans


def mix_forward(filtered, weights, channels):
    zero_rows = 5 * channels
    pieces = [jnp.dot(weights[0], filtered[:zero_rows], preferred_element_type=jnp.float32)]
    for number, (begin_row, mid_row, end_row) in enumerate(order_spans(channels)):
        matrix = weights[number + 1]
        plus_rows = filtered[begin_row:mid_row]
        minus_rows = filtered[mid_row:end_row]
        pieces.append(jnp.dot(matrix[0], plus_rows, preferred_element_type=jnp.float32)
                      - jnp.dot(matrix[1], minus_rows, preferred_element_type=jnp.float32))
        pieces.append(jnp.dot(matrix[1], plus_rows, preferred_element_type=jnp.float32)
                      + jnp.dot(matrix[0], minus_rows, preferred_element_type=jnp.float32))
    return jnp.concatenate(pieces, axis=0)


def mix_backward(grads_in, weights, channels):
    zero_rows = 5 * channels
    pieces = [jnp.dot(weights[0].T, grads_in[:zero_rows], preferred_element_type=jnp.float32)]
    for number, (begin_row, mid_row, end_row) in enumerate(order_spans(channels)):
        matrix = weights[number + 1]
        plus_rows = grads_in[begin_row:mid_row]
        minus_rows = grads_in[mid_row:end_row]
        pieces.append(jnp.dot(matrix[0].T, plus_rows, preferred_element_type=jnp.float32)
                      + jnp.dot(matrix[1].T, minus_rows, preferred_element_type=jnp.float32))
        pieces.append(jnp.dot(matrix[0].T, minus_rows, preferred_element_type=jnp.float32)
                      - jnp.dot(matrix[1].T, plus_rows, preferred_element_type=jnp.float32))
    return jnp.concatenate(pieces, axis=0)


def apply_harmonics(columns, harmonics, channels):
    edge_count = columns.shape[1]
    shaped = columns.astype(jnp.float32).reshape(25, channels, edge_count)
    return (shaped * harmonics[:, None, :]).reshape(25 * channels, edge_count)


def edge_forward(extended, sources, targets, harmonics, weights, atoms, blocks_used):
    feature_rows = extended.shape[0]
    channels = feature_rows // 25

    def visit_block(block_id, running):
        row_begin = block_id * EDGE_BLOCK
        source_ids = lax.dynamic_slice_in_dim(sources, row_begin, EDGE_BLOCK)
        target_ids = lax.dynamic_slice_in_dim(targets, row_begin, EDGE_BLOCK)
        harmonic_block = lax.dynamic_slice_in_dim(harmonics, row_begin, EDGE_BLOCK, 1)
        columns = jnp.take(extended, source_ids, axis=1)
        filtered = apply_harmonics(columns, harmonic_block, channels).astype(jnp.bfloat16)
        message = mix_forward(filtered, weights, channels)
        return running.at[:, target_ids].add(message, mode="drop")

    start_sum = jnp.zeros((feature_rows, atoms), jnp.float32)
    return lax.fori_loop(0, blocks_used, visit_block, start_sum)


def edge_backward(d_aggregate, sources, targets, harmonics, weights, extended_cols, blocks_used):
    feature_rows = d_aggregate.shape[0]
    channels = feature_rows // 25

    def visit_block(block_id, running):
        row_begin = block_id * EDGE_BLOCK
        source_ids = lax.dynamic_slice_in_dim(sources, row_begin, EDGE_BLOCK)
        target_ids = lax.dynamic_slice_in_dim(targets, row_begin, EDGE_BLOCK)
        harmonic_block = lax.dynamic_slice_in_dim(harmonics, row_begin, EDGE_BLOCK, 1)
        grads_in = jnp.take(d_aggregate, target_ids, axis=1, mode="fill", fill_value=0)
        d_filtered = mix_backward(grads_in, weights, channels)
        d_source = apply_harmonics(d_filtered, harmonic_block, channels)
        return running.at[:, source_ids].add(d_source)

    start_sum = jnp.zeros((feature_rows, extended_cols), jnp.float32)
    return lax.fori_loop(0, blocks_used, visit_block, start_sum)


def node_forward(features, aggregate, to_grid, from_grid):
    channels = features.shape[0] // 25
    atoms = features.shape[1]
    scaled = (aggregate * edge_norm).reshape(25, channels, atoms)
    feature_f32 = features.astype(jnp.float32).reshape(25, channels, atoms)
    grid_agg = jnp.einsum("gk,kca->gca", to_grid, scaled, precision=lax.Precision.HIGHEST)
    grid_feat = jnp.einsum("gk,kca->gca", to_grid, feature_f32, precision=lax.Precision.HIGHEST)
    sigmoid_agg = jax.nn.sigmoid(grid_agg)
    activated = grid_agg * sigmoid_agg
    update = jnp.einsum("kg,gca->kca", from_grid, activated * grid_feat, precision=lax.Precision.HIGHEST)
    layer_out = (feature_f32 + update).reshape(25 * channels, atoms).astype(jnp.bfloat16)
    return layer_out, (grid_agg, grid_feat, sigmoid_agg, activated)


def node_backward(cotangent, saved, to_grid, from_grid):
    grid_agg, grid_feat, sigmoid_agg, activated = saved
    channels = cotangent.shape[0] // 25
    atoms = cotangent.shape[1]
    cot_f32 = cotangent.astype(jnp.float32).reshape(25, channels, atoms)
    d_product = jnp.einsum("kg,kca->gca", from_grid, cot_f32, precision=lax.Precision.HIGHEST)
    d_grid_agg = d_product * grid_feat * (sigmoid_agg * (1.0 + grid_agg * (1.0 - sigmoid_agg)))
    d_grid_feat = d_product * activated
    node_grad = cot_f32 + jnp.einsum("gk,gca->kca", to_grid, d_grid_feat, precision=lax.Precision.HIGHEST)
    d_aggregate = jnp.einsum("gk,gca->kca", to_grid, d_grid_agg, precision=lax.Precision.HIGHEST) * edge_norm
    d_aggregate = d_aggregate.reshape(25 * channels, atoms).astype(jnp.bfloat16)
    return node_grad.reshape(25 * channels, atoms), d_aggregate


def pick_columns(matrix, indices):
    return jnp.take(matrix, indices, axis=1)


def add_columns(matrix, indices, values):
    return matrix.at[:, indices].add(values)


def reference(features, cotangent, w_order0, w_order1, w_order2, w_order3, w_order4, to_grid, from_grid, edge_harmonics, edge_source, edge_target, send_list):
    weights = (w_order0, w_order1, w_order2, w_order3, w_order4)
    grid_x = features.shape[0]
    grid_y = features.shape[1]
    feature_rows = features.shape[2]
    atoms = features.shape[3]
    ghost_width = send_list.shape[3]
    ghost_blocks = []
    for index, (shift_x, shift_y) in enumerate(DIRECTIONS):
        moved_feat = jnp.roll(features, (-shift_x, -shift_y), axis=(0, 1))
        moved_list = jnp.roll(send_list[:, :, index], (-shift_x, -shift_y), axis=(0, 1))
        ghost_blocks.append(jax.vmap(jax.vmap(pick_columns))(moved_feat, moved_list))
    ghosts = jnp.concatenate(ghost_blocks, axis=3)

    def flatten_cells(array):
        return array.reshape((grid_x * grid_y,) + array.shape[2:])

    def per_cell(packed):
        own, ghost_cols, cot_cell, sources, targets, harmonics = packed
        extended = jnp.concatenate([own, ghost_cols], axis=1)
        live_count = jnp.sum((targets < atoms).astype(jnp.int32)).astype(jnp.int32)
        blocks_used = ((live_count + EDGE_BLOCK - 1) // EDGE_BLOCK).astype(jnp.int32)
        aggregate = edge_forward(extended, sources, targets, harmonics, weights, atoms, blocks_used)
        layer_cell, saved = node_forward(own, aggregate, to_grid, from_grid)
        node_grad, d_aggregate = node_backward(cot_cell, saved, to_grid, from_grid)
        d_extended = edge_backward(d_aggregate, sources, targets, harmonics, weights, extended.shape[1], blocks_used)
        return layer_cell, node_grad + d_extended[:, :atoms], d_extended[:, atoms:]

    packed_all = (flatten_cells(features), flatten_cells(ghosts), flatten_cells(cotangent),
                  flatten_cells(edge_source), flatten_cells(edge_target), flatten_cells(edge_harmonics))
    results = lax.map(per_cell, packed_all)
    layer_out = results[0].reshape(features.shape)
    local_grad = results[1].reshape(features.shape)
    ghost_grad = results[2].reshape(grid_x, grid_y, feature_rows, 8 * ghost_width)
    for index, (shift_x, shift_y) in enumerate(DIRECTIONS):
        piece = ghost_grad[:, :, :, index * ghost_width:(index + 1) * ghost_width]
        moved = jnp.roll(piece, (shift_x, shift_y), axis=(0, 1))
        local_grad = jax.vmap(jax.vmap(add_columns))(local_grad, send_list[:, :, index], moved)
    return layer_out, local_grad
```

```python
import functools

import jax
import jax.numpy as jnp
from jax import lax
from jax.experimental import pallas as pl
from jax.experimental.pallas import tpu as pltpu
from jax.sharding import PartitionSpec as P


F32, BF16, I32 = jnp.float32, jnp.bfloat16, jnp.int32
COEFS = 25
DEGREES = 5
edge_norm = 0.35
SWAPS = ((1, 1), (1, 0), (1, None), (0, 1), (0, 0), (0, None), (None, 1), (None, 0))


def step_of(axis, parity):
    if parity is None:
        return 0
    return jnp.where(lax.rem(lax.axis_index(axis), 2) == parity, 1, -1)


def received_direction(swap):
    place = 3 * (step_of("gx", swap[0]) + 1) + step_of("gy", swap[1]) + 1
    return place - jnp.where(place > 4, 1, 0)


def traded(value, swap):
    nx, ny = lax.axis_size("gx"), lax.axis_size("gy")

    def partner(place, size, parity):
        if parity is None:
            return place
        return (place + (1 if place % 2 == parity else -1)) % size

    pairs = [
        (x * ny + y, partner(x, nx, swap[0]) * ny + partner(y, ny, swap[1]))
        for x in range(nx)
        for y in range(ny)
    ]
    return lax.ppermute(value, ("gx", "gy"), pairs)


def iota(shape, axis):
    return lax.broadcasted_iota(I32, shape, axis)


def dot(a, b):
    return jnp.dot(a, b, preferred_element_type=F32)


def dot_nt(a, b):
    return lax.dot_general(a, b, (((1,), (1,)), ((), ())), preferred_element_type=F32)


def dot_tn(a, b):
    return lax.dot_general(a, b, (((0,), (0,)), ((), ())), preferred_element_type=F32)


def split(value):
    high = value.astype(BF16)
    return high, (value - high.astype(F32)).astype(BF16)


def rows_of(value, part):
    rows, width = value.shape
    quarter = rows // COEFS // 4
    return value.reshape(COEFS, 4, quarter, width)[:, part].reshape(COEFS * quarter, width)


def lane_group(shape):
    return lax.shift_right_logical(iota(shape, 1), 5)


def merged(blocks, part):
    group = lane_group((1, 128))
    result = blocks[(3 - part) % 4]
    for m in range(3):
        result = jnp.where(group == m, blocks[(m - part) % 4], result)
    return result


def pack_kernel(own_ref, lists_ref, *refs):
    outs, scratch = refs[:8], refs[8]
    place = iota((8, 8), 0)
    wanted = jnp.zeros((8, 8), I32)
    for s, swap in enumerate(SWAPS):
        wanted = jnp.where(place == s, 7 - received_direction(swap), wanted)
    order = (wanted == iota((8, 8), 1)).astype(BF16)
    spread = (lax.bitwise_and(iota((32, 128), 1), 31) == iota((32, 128), 0)).astype(BF16)
    chosen = dot(order, lists_ref[...].astype(F32).astype(BF16)).astype(BF16)
    lists = dot(chosen, spread).astype(I32)
    atom = iota((128, 256), 0)
    own = own_ref[...]
    for q in range(4):
        row = jnp.concatenate(
            [merged([lists[4 * g + k : 4 * g + k + 1] for k in range(4)], q) for g in range(2)], axis=1
        )
        scratch[q] = dot(rows_of(own, q), (atom == row).astype(BF16))
    for g in range(2):
        for k in range(4):
            parts = [scratch[q, :, 128 * g : 128 * g + 128] for q in range(4)]
            outs[4 * g + k][...] = merged(parts, k).astype(BF16)


def spread_rows(count, inner):
    shape = (count * 8, count)
    return (lax.shift_right_logical(iota(shape, 0), 3) == iota(shape, 1)).astype(BF16)


def spread_cols(count):
    shape = (count, count * 8)
    return (lax.shift_right_logical(iota(shape, 1), 3) == iota(shape, 0)).astype(BF16)


def diagonal(shape):
    return lax.bitwise_and(iota(shape, 0), 7) == lax.bitwise_and(iota(shape, 1), 7)


def widen(left, right):
    wide = dot(left.astype(BF16), right)
    return jnp.where(diagonal(wide.shape), wide, 0.0).astype(BF16)


def channel_pair(value, p):
    width = value.shape[1]
    shaped = value.reshape(COEFS, value.shape[0] // COEFS // 8, 8, width)
    return jnp.concatenate(
        [shaped[:, 2 * p + h].reshape(COEFS * 8, width) for h in range(2)], axis=1
    )


def local_kernel(own_ref, cot_ref, to_ref, from_ref, feat_ref, prod_ref, up_ref, down_ref, fdown_ref):
    points = to_ref.shape[0]
    to_parts, from_parts = split(to_ref[...]), split(from_ref[...])
    ups, fups = [], []
    for n in range(2):
        ups.append(widen(dot(spread_rows(points, 8), to_parts[n]), spread_cols(COEFS)))
        fups.append(widen(dot_nt(spread_rows(points, 8), from_parts[n]), spread_cols(COEFS)))
        up_ref[n] = ups[n]
        down_ref[n] = widen(dot_nt(spread_rows(COEFS, 8), to_parts[n]), spread_cols(points))
        fdown_ref[n] = widen(dot(spread_rows(COEFS, 8), from_parts[n]), spread_cols(points))
    own = own_ref[...].astype(F32)
    cot = cot_ref[...].astype(F32)
    for p in range(own.shape[0] // COEFS // 16):
        x = channel_pair(own, p).astype(BF16)
        feat_ref[p] = dot(ups[0], x) + dot(ups[1], x)
        x = channel_pair(cot, p).astype(BF16)
        prod_ref[p] = dot(fups[0], x) + dot(fups[1], x)


def order_spans(channels):
    spans = []
    offset = DEGREES * channels
    for gap in range(1, DEGREES):
        length = (DEGREES - gap) * channels
        spans.append((offset, offset + length, offset + 2 * length))
        offset += 2 * length
    return spans


def folded(value):
    half = value.shape[1] // 2
    return value[:, :half] + value[:, half:]


def edge_kernel(*refs):
    ghosts = refs[:8]
    own_ref, src_ref, tgt_ref, harm_ref, w0_ref, w1_ref, w2_ref, w3_ref, w4_ref = refs[8:17]
    feat_ref, prod_ref, up_ref, down_ref = refs[17:21]
    outs = refs[21:29]
    act_ref, dfeat_ref, dsrc_ref = refs[29:32]
    filt, mixed, agg, dagg, packed = refs[32:]
    channels = own_ref.shape[0] // COEFS
    quarter = channels // 4
    edges = src_ref.shape[1]
    atoms = own_ref.shape[1]
    weights = (w1_ref, w2_ref, w3_ref, w4_ref)
    src = src_ref[...]
    tgt = tgt_ref[...]
    own_pick = (iota((atoms, edges), 0) == src).astype(BF16)
    target_pick = (iota((atoms, edges), 0) == tgt).astype(BF16)
    slabs = []
    for swap in SWAPS:
        base = atoms + 32 * received_direction(swap)
        slabs.append((iota((32, edges), 0) + base == src).astype(BF16))
    picks = [
        jnp.concatenate([slabs[4 * g + (m - q) % 4] for g in range(2) for m in range(4)], axis=0)
        for q in range(4)
    ]
    own = own_ref[...]
    blocks = [ghosts[s][...] for s in range(8)]
    for q in range(4):
        taken = jnp.concatenate([merged(blocks[4 * g : 4 * g + 4], q) for g in range(2)], axis=1)
        columns = dot(taken, picks[q]) + dot(rows_of(own, q), own_pick)
        scaled = columns.reshape(COEFS, quarter, edges) * harm_ref[...]
        filt[:, q * quarter : (q + 1) * quarter] = scaled.astype(BF16)
    summed = dot_nt(filt[...].reshape(COEFS * channels, edges), target_pick)
    high, low = split(summed)
    mixed[:, :atoms] = high
    mixed[:, atoms:] = low
    zero_rows = DEGREES * channels
    agg[:zero_rows] = folded(dot(w0_ref[...], mixed[:zero_rows])) * edge_norm
    for w, (begin, mid, end) in zip(weights, order_spans(channels)):
        plus, minus = mixed[begin:mid], mixed[mid:end]
        agg[begin:mid] = folded(dot(w[0], plus) - dot(w[1], minus)) * edge_norm
        agg[mid:end] = folded(dot(w[1], plus) + dot(w[0], minus)) * edge_norm
    for p in range(channels // 16):
        xh, xl = split(channel_pair(agg[...], p))
        grid_agg = dot(up_ref[0], xh) + dot(up_ref[0], xl) + dot(up_ref[1], xh)
        sig = jax.nn.sigmoid(grid_agg)
        act = grid_agg * sig
        feat, dprod = feat_ref[p], prod_ref[p]
        act_ref[p] = act * feat
        dfeat_ref[p] = dprod * act
        dh, dl = split(dprod * feat * (sig + act * (1.0 - sig)))
        down = (dot(down_ref[0], dh) + dot(down_ref[0], dl) + dot(down_ref[1], dh)) * edge_norm
        for h in range(2):
            dagg[:, 2 * p + h] = down[:, h * atoms : (h + 1) * atoms].reshape(COEFS, 8, atoms)
    back = dagg[...].reshape(COEFS * channels, atoms).astype(BF16)

    def keep(rows, value):
        high, low = split(value)
        mixed[rows, :atoms] = high
        mixed[rows, atoms:] = low

    keep(slice(0, zero_rows), dot_tn(w0_ref[...], back[:zero_rows]))
    for w, (begin, mid, end) in zip(weights, order_spans(channels)):
        plus, minus = back[begin:mid], back[mid:end]
        keep(slice(begin, mid), dot_tn(w[0], plus) + dot_tn(w[1], minus))
        keep(slice(mid, end), dot_tn(w[0], minus) - dot_tn(w[1], plus))
    both = jnp.concatenate([target_pick, target_pick], axis=0)
    for q in range(4):
        grads = dot(rows_of(mixed[...], q), both)
        scaled = (grads.reshape(COEFS, quarter, edges) * harm_ref[...]).reshape(COEFS * quarter, edges)
        high, low = split(scaled)
        dsrc_ref[0, q] = high
        dsrc_ref[1, q] = low
        packed[q] = dot_nt(high, picks[q]) + dot_nt(low, picks[q])
    for g in range(2):
        for k in range(4):
            parts = [packed[q, :, 128 * g : 128 * g + 128] for q in range(4)]
            outs[4 * g + k][...] = merged(parts, k).astype(BF16)


def after_kernel(own_ref, cot_ref, src_ref, down_ref, fdown_ref, act_ref, dfeat_ref, dsrc_ref, out_ref, grad_ref):
    rows, atoms = own_ref.shape
    channels = rows // COEFS
    quarter = channels // 4
    edges = src_ref.shape[1]
    own_pick = (iota((atoms, edges), 0) == src_ref[...]).astype(BF16)
    own = own_ref[...].astype(F32).reshape(COEFS, channels // 8, 8, atoms)
    cot = cot_ref[...].astype(F32).reshape(COEFS, channels // 8, 8, atoms)
    local = [dot_nt(dsrc_ref[0, q], own_pick) + dot_nt(dsrc_ref[1, q], own_pick) for q in range(4)]
    for p in range(channels // 16):
        ah, al = split(act_ref[p])
        update = dot(fdown_ref[0], ah) + dot(fdown_ref[0], al) + dot(fdown_ref[1], ah)
        ah, al = split(dfeat_ref[p])
        grad = dot(down_ref[0], ah) + dot(down_ref[0], al) + dot(down_ref[1], ah)
        here = local[p].reshape(COEFS, 2, 8, atoms)
        outs = []
        for h in range(2):
            lanes = slice(h * atoms, (h + 1) * atoms)
            outs.append(own[:, 2 * p + h] + update[:, lanes].reshape(COEFS, 8, atoms))
            grad_ref[:, 2 * p + h] = (
                cot[:, 2 * p + h] + grad[:, lanes].reshape(COEFS, 8, atoms) + here[:, h]
            )
        out_ref[:, p] = jnp.concatenate(outs, axis=1).astype(BF16)


def final_kernel(*refs):
    blocks = [r[...] for r in refs[:8]]
    lists_ref, grad_ref, out_ref = refs[8:]
    place = iota((8, 8), 0)
    wanted = jnp.zeros((8, 8), I32)
    for s, swap in enumerate(SWAPS):
        wanted = jnp.where(place == s, 7 - received_direction(swap), wanted)
    order = (wanted == iota((8, 8), 1)).astype(BF16)
    spread = (lax.bitwise_and(iota((32, 128), 1), 31) == iota((32, 128), 0)).astype(BF16)
    chosen = dot(order, lists_ref[...].astype(F32).astype(BF16)).astype(BF16)
    lists = dot(chosen, spread).astype(I32)
    atom = iota((128, 256), 0)
    for q in range(4):
        row = jnp.concatenate(
            [merged([lists[4 * g + k : 4 * g + k + 1] for k in range(4)], q) for g in range(2)], axis=1
        )
        taken = jnp.concatenate([merged(blocks[4 * g : 4 * g + 4], q) for g in range(2)], axis=1)
        added = dot_nt(taken, (atom == row).astype(BF16))
        quarter = added.shape[0] // COEFS
        rows = slice(q * quarter, (q + 1) * quarter)
        out_ref[:, rows] = grad_ref[:, rows] + added.reshape(COEFS, quarter, 128)


VM = pl.BlockSpec(memory_space=pltpu.VMEM)


def call(kernel, outs, scratch=()):
    def run(*args):
        return pl.pallas_call(
            kernel,
            out_shape=outs,
            in_specs=[VM] * len(args),
            out_specs=jax.tree.map(lambda _: VM, outs),
            scratch_shapes=list(scratch),
            compiler_params=pltpu.CompilerParams(vmem_limit_bytes=60 * 1024 * 1024),
        )(*args)

    return run


def per_device(
    features,
    cotangent,
    w_order0,
    w_order1,
    w_order2,
    w_order3,
    w_order4,
    to_grid,
    from_grid,
    edge_harmonics,
    edge_source,
    edge_target,
    send_list,
):
    own = features[0, 0]
    cot = cotangent[0, 0]
    rows, atoms = own.shape
    channels = rows // COEFS
    edges = edge_source.shape[2]
    points = to_grid.shape[0]
    pairs = channels // 16
    lists = send_list[0, 0]
    src, tgt = edge_source[0], edge_target[0]
    harm = edge_harmonics[0, 0][:, None, :]
    like = jax.ShapeDtypeStruct
    block = like((rows // 4, atoms), BF16)
    grid = like((pairs, points * 8, 2 * atoms), F32)
    packed = call(
        pack_kernel, [block] * 8, [pltpu.VMEM((4, rows // 4, 2 * atoms), F32)]
    )(own, lists)
    ghosts = [traded(packed[s], swap) for s, swap in enumerate(SWAPS)]
    feat, prod, up, down, fdown = call(
        local_kernel,
        [
            grid,
            grid,
            like((2, points * 8, COEFS * 8), BF16),
            like((2, COEFS * 8, points * 8), BF16),
            like((2, COEFS * 8, points * 8), BF16),
        ],
    )(own, cot, to_grid, from_grid)
    results = call(
        edge_kernel,
        [block] * 8 + [grid, grid, like((2, 4, rows // 4, edges), BF16)],
        [
            pltpu.VMEM((COEFS, channels, edges), BF16),
            pltpu.VMEM((rows, 2 * atoms), BF16),
            pltpu.VMEM((rows, atoms), F32),
            pltpu.VMEM((COEFS, channels // 8, 8, atoms), F32),
            pltpu.VMEM((4, rows // 4, 2 * atoms), F32),
        ],
    )(*ghosts, own, src, tgt, harm, w_order0, w_order1, w_order2, w_order3, w_order4, feat, prod, up, down)
    returning = [traded(results[s], swap) for s, swap in enumerate(SWAPS)]
    act, dfeat, dsrc = results[8:]
    layer, grad = call(
        after_kernel,
        [like((COEFS, pairs, 16, atoms), BF16), like((COEFS, channels // 8, 8, atoms), F32)],
    )(own, cot, src, down, fdown, act, dfeat, dsrc)
    total = call(final_kernel, like((COEFS, channels, atoms), F32))(
        *returning, lists, grad.reshape(COEFS, channels, atoms)
    )
    return layer.reshape(1, 1, rows, atoms), total.reshape(1, 1, rows, atoms)


def solution(mesh):
    cell = P("gx", "gy", None, None)
    row = P("gx", "gy", None)
    placed = (cell, cell, P(), P(), P(), P(), P(), P(), P(), cell, row, row, cell)
    return jax.shard_map(
        per_device, mesh=mesh, in_specs=placed, out_specs=(cell, cell), check_vma=False
    )
```

```python
import functools

import jax
import jax.numpy as jnp
from jax import lax
from jax.experimental import pallas as pl
from jax.experimental.pallas import tpu as pltpu
from jax.sharding import PartitionSpec as P


F32, BF16, I32 = jnp.float32, jnp.bfloat16, jnp.int32
COEFS = 25
DEGREES = 5
edge_norm = 0.35
SWAPS = ((1, 1), (1, 0), (1, None), (0, 1), (0, 0), (0, None), (None, 1), (None, 0))


def step_of(axis, parity):
    if parity is None:
        return 0
    return jnp.where(lax.rem(lax.axis_index(axis), 2) == parity, 1, -1)


def received_direction(swap):
    place = 3 * (step_of("gx", swap[0]) + 1) + step_of("gy", swap[1]) + 1
    return place - jnp.where(place > 4, 1, 0)


def traded(value, swap):
    nx, ny = lax.axis_size("gx"), lax.axis_size("gy")

    def partner(place, size, parity):
        if parity is None:
            return place
        return (place + (1 if place % 2 == parity else -1)) % size

    pairs = [
        (x * ny + y, partner(x, nx, swap[0]) * ny + partner(y, ny, swap[1]))
        for x in range(nx)
        for y in range(ny)
    ]
    return lax.ppermute(value, ("gx", "gy"), pairs)


def iota(shape, axis):
    return lax.broadcasted_iota(I32, shape, axis)


def dot(a, b):
    return jnp.dot(a, b, preferred_element_type=F32)


def dot_nt(a, b):
    return lax.dot_general(a, b, (((1,), (1,)), ((), ())), preferred_element_type=F32)


def dot_tn(a, b):
    return lax.dot_general(a, b, (((0,), (0,)), ((), ())), preferred_element_type=F32)


def split(value):
    high = value.astype(BF16)
    return high, (value - high.astype(F32)).astype(BF16)


def rows_of(value, part):
    rows, width = value.shape
    quarter = rows // COEFS // 4
    return value.reshape(COEFS, 4, quarter, width)[:, part].reshape(COEFS * quarter, width)


def lane_group(shape):
    return lax.shift_right_logical(iota(shape, 1), 5)


def merged(blocks, part):
    group = lane_group((1, 128))
    result = blocks[(3 - part) % 4]
    for m in range(3):
        result = jnp.where(group == m, blocks[(m - part) % 4], result)
    return result


def fetch(sources, targets, sems):
    copies = [pltpu.make_async_copy(a, b, sems.at[n]) for n, (a, b) in enumerate(zip(sources, targets))]
    for copy in copies:
        copy.start()
    return copies


def pack_kernel(own_hbm, lists_hbm, *refs):
    outs, own_ref, lists_ref, scratch, sems = refs[:8], refs[8], refs[9], refs[10], refs[11]
    copies = fetch((lists_hbm, own_hbm), (lists_ref, own_ref), sems)
    copies[0].wait()
    place = iota((8, 8), 0)
    wanted = jnp.zeros((8, 8), I32)
    for s, swap in enumerate(SWAPS):
        wanted = jnp.where(place == s, 7 - received_direction(swap), wanted)
    order = (wanted == iota((8, 8), 1)).astype(BF16)
    spread = (lax.bitwise_and(iota((32, 128), 1), 31) == iota((32, 128), 0)).astype(BF16)
    chosen = dot(order, lists_ref[...].astype(F32).astype(BF16)).astype(BF16)
    lists = dot(chosen, spread).astype(I32)
    atom = iota((128, 256), 0)
    copies[1].wait()
    own = own_ref[...]
    for q in range(4):
        row = jnp.concatenate(
            [merged([lists[4 * g + k : 4 * g + k + 1] for k in range(4)], q) for g in range(2)], axis=1
        )
        scratch[q] = dot(rows_of(own, q), (atom == row).astype(BF16))
    for g in range(2):
        for k in range(4):
            parts = [scratch[q, :, 128 * g : 128 * g + 128] for q in range(4)]
            outs[4 * g + k][...] = merged(parts, k).astype(BF16)


def spread_rows(count, inner):
    shape = (count * 8, count)
    return (lax.shift_right_logical(iota(shape, 0), 3) == iota(shape, 1)).astype(BF16)


def spread_cols(count):
    shape = (count, count * 8)
    return (lax.shift_right_logical(iota(shape, 1), 3) == iota(shape, 0)).astype(BF16)


def diagonal(shape):
    return lax.bitwise_and(iota(shape, 0), 7) == lax.bitwise_and(iota(shape, 1), 7)


def widen(left, right):
    wide = dot(left.astype(BF16), right)
    return jnp.where(diagonal(wide.shape), wide, 0.0).astype(BF16)


def channel_pair(value, p):
    width = value.shape[1]
    shaped = value.reshape(COEFS, value.shape[0] // COEFS // 8, 8, width)
    return jnp.concatenate(
        [shaped[:, 2 * p + h].reshape(COEFS * 8, width) for h in range(2)], axis=1
    )


def local_kernel(own_ref, *refs):
    given, refs = refs[:11], refs[11:]
    feat_ref, prod_ref, up_ref, down_ref, fdown_ref = refs[:5]
    kept, refs = refs[5:14], refs[14:]
    to_ref, from_ref, sems = refs
    copies = fetch(given, (to_ref, from_ref, *kept), sems)
    cot_ref = kept[0]
    copies[0].wait()
    copies[1].wait()
    points = to_ref.shape[1]
    to_parts, from_parts = split(to_ref[...]), split(from_ref[...])
    ups, fups = [], []
    for n in range(2):
        ups.append(widen(dot_nt(spread_rows(points, 8), to_parts[n]), spread_cols(COEFS)))
        fups.append(widen(dot_nt(spread_rows(points, 8), from_parts[n]), spread_cols(COEFS)))
        up_ref[n] = ups[n]
        down_ref[n] = widen(dot(spread_rows(COEFS, 8), to_parts[n]), spread_cols(points))
        fdown_ref[n] = widen(dot(spread_rows(COEFS, 8), from_parts[n]), spread_cols(points))
    own = own_ref[...].astype(F32)
    pairs = own.shape[0] // COEFS // 16
    for p in range(pairs):
        x = channel_pair(own, p).astype(BF16)
        feat_ref[p] = dot(ups[0], x) + dot(ups[1], x)
    for copy in copies[2:]:
        copy.wait()
    cot = cot_ref[...].astype(F32)
    for p in range(pairs):
        x = channel_pair(cot, p).astype(BF16)
        prod_ref[p] = dot(fups[0], x) + dot(fups[1], x)


def order_spans(channels):
    spans = []
    offset = DEGREES * channels
    for gap in range(1, DEGREES):
        length = (DEGREES - gap) * channels
        spans.append((offset, offset + length, offset + 2 * length))
        offset += 2 * length
    return spans


def folded(value):
    half = value.shape[1] // 2
    return value[:, :half] + value[:, half:]


def edge_kernel(*refs):
    ghosts = refs[:8]
    own_ref, src_ref, tgt_ref, harm_ref, w0_ref, w1_ref, w2_ref, w3_ref, w4_ref = refs[8:17]
    feat_ref, prod_ref, up_ref, down_ref = refs[17:21]
    outs = refs[21:29]
    act_ref, dfeat_ref, dsrc_ref = refs[29:32]
    filt, mixed, agg, dagg, packed = refs[32:]
    channels = own_ref.shape[0] // COEFS
    quarter = channels // 4
    edges = src_ref.shape[1]
    atoms = own_ref.shape[1]
    weights = (w1_ref, w2_ref, w3_ref, w4_ref)
    src = src_ref[...]
    tgt = tgt_ref[...]
    own_pick = (iota((atoms, edges), 0) == src).astype(BF16)
    target_pick = (iota((atoms, edges), 0) == tgt).astype(BF16)
    slabs = []
    for swap in SWAPS:
        base = atoms + 32 * received_direction(swap)
        slabs.append((iota((32, edges), 0) + base == src).astype(BF16))
    picks = [
        jnp.concatenate([slabs[4 * g + (m - q) % 4] for g in range(2) for m in range(4)], axis=0)
        for q in range(4)
    ]
    own = own_ref[...]
    blocks = [ghosts[s][...] for s in range(8)]
    for q in range(4):
        taken = jnp.concatenate([merged(blocks[4 * g : 4 * g + 4], q) for g in range(2)], axis=1)
        columns = dot(taken, picks[q]) + dot(rows_of(own, q), own_pick)
        scaled = columns.reshape(COEFS, quarter, edges) * harm_ref[...]
        filt[:, q * quarter : (q + 1) * quarter] = scaled.astype(BF16)
    summed = dot_nt(filt[...].reshape(COEFS * channels, edges), target_pick)
    high, low = split(summed)
    mixed[:, :atoms] = high
    mixed[:, atoms:] = low
    zero_rows = DEGREES * channels
    agg[:zero_rows] = folded(dot(w0_ref[...], mixed[:zero_rows])) * edge_norm
    for w, (begin, mid, end) in zip(weights, order_spans(channels)):
        plus, minus = mixed[begin:mid], mixed[mid:end]
        agg[begin:mid] = folded(dot(w[0], plus) - dot(w[1], minus)) * edge_norm
        agg[mid:end] = folded(dot(w[1], plus) + dot(w[0], minus)) * edge_norm
    for p in range(channels // 16):
        xh, xl = split(channel_pair(agg[...], p))
        grid_agg = dot(up_ref[0], xh) + dot(up_ref[0], xl) + dot(up_ref[1], xh)
        sig = jax.nn.sigmoid(grid_agg)
        act = grid_agg * sig
        feat, dprod = feat_ref[p], prod_ref[p]
        act_ref[p] = act * feat
        dfeat_ref[p] = dprod * act
        dh, dl = split(dprod * feat * (sig + act * (1.0 - sig)))
        down = (dot(down_ref[0], dh) + dot(down_ref[0], dl) + dot(down_ref[1], dh)) * edge_norm
        for h in range(2):
            dagg[:, 2 * p + h] = down[:, h * atoms : (h + 1) * atoms].reshape(COEFS, 8, atoms)
    back = dagg[...].reshape(COEFS * channels, atoms).astype(BF16)

    def keep(rows, value):
        high, low = split(value)
        mixed[rows, :atoms] = high
        mixed[rows, atoms:] = low

    keep(slice(0, zero_rows), dot_tn(w0_ref[...], back[:zero_rows]))
    for w, (begin, mid, end) in zip(weights, order_spans(channels)):
        plus, minus = back[begin:mid], back[mid:end]
        keep(slice(begin, mid), dot_tn(w[0], plus) + dot_tn(w[1], minus))
        keep(slice(mid, end), dot_tn(w[0], minus) - dot_tn(w[1], plus))
    both = jnp.concatenate([target_pick, target_pick], axis=0)
    for q in range(4):
        grads = dot(rows_of(mixed[...], q), both)
        scaled = (grads.reshape(COEFS, quarter, edges) * harm_ref[...]).reshape(COEFS * quarter, edges)
        high, low = split(scaled)
        dsrc_ref[0, q] = high
        dsrc_ref[1, q] = low
        packed[q] = dot_nt(high, picks[q]) + dot_nt(low, picks[q])
    for g in range(2):
        for k in range(4):
            parts = [packed[q, :, 128 * g : 128 * g + 128] for q in range(4)]
            outs[4 * g + k][...] = merged(parts, k).astype(BF16)


def after_kernel(own_ref, cot_ref, src_ref, down_ref, fdown_ref, act_ref, dfeat_ref, dsrc_ref, out_ref, grad_ref):
    rows, atoms = own_ref.shape
    channels = rows // COEFS
    quarter = channels // 4
    edges = src_ref.shape[1]
    own_pick = (iota((atoms, edges), 0) == src_ref[...]).astype(BF16)
    own = own_ref[...].astype(F32).reshape(COEFS, channels // 8, 8, atoms)
    cot = cot_ref[...].astype(F32).reshape(COEFS, channels // 8, 8, atoms)
    local = [dot_nt(dsrc_ref[0, q], own_pick) + dot_nt(dsrc_ref[1, q], own_pick) for q in range(4)]
    for p in range(channels // 16):
        ah, al = split(act_ref[p])
        update = dot(fdown_ref[0], ah) + dot(fdown_ref[0], al) + dot(fdown_ref[1], ah)
        ah, al = split(dfeat_ref[p])
        grad = dot(down_ref[0], ah) + dot(down_ref[0], al) + dot(down_ref[1], ah)
        here = local[p].reshape(COEFS, 2, 8, atoms)
        outs = []
        for h in range(2):
            lanes = slice(h * atoms, (h + 1) * atoms)
            outs.append(own[:, 2 * p + h] + update[:, lanes].reshape(COEFS, 8, atoms))
            grad_ref[:, 2 * p + h] = (
                cot[:, 2 * p + h] + grad[:, lanes].reshape(COEFS, 8, atoms) + here[:, h]
            )
        out_ref[:, p] = jnp.concatenate(outs, axis=1).astype(BF16)


def final_kernel(*refs):
    blocks = [r[...] for r in refs[:8]]
    lists_ref, grad_ref, out_ref = refs[8:]
    place = iota((8, 8), 0)
    wanted = jnp.zeros((8, 8), I32)
    for s, swap in enumerate(SWAPS):
        wanted = jnp.where(place == s, 7 - received_direction(swap), wanted)
    order = (wanted == iota((8, 8), 1)).astype(BF16)
    spread = (lax.bitwise_and(iota((32, 128), 1), 31) == iota((32, 128), 0)).astype(BF16)
    chosen = dot(order, lists_ref[...].astype(F32).astype(BF16)).astype(BF16)
    lists = dot(chosen, spread).astype(I32)
    atom = iota((128, 256), 0)
    for q in range(4):
        row = jnp.concatenate(
            [merged([lists[4 * g + k : 4 * g + k + 1] for k in range(4)], q) for g in range(2)], axis=1
        )
        taken = jnp.concatenate([merged(blocks[4 * g : 4 * g + 4], q) for g in range(2)], axis=1)
        added = dot_nt(taken, (atom == row).astype(BF16))
        quarter = added.shape[0] // COEFS
        rows = slice(q * quarter, (q + 1) * quarter)
        out_ref[:, rows] = grad_ref[:, rows] + added.reshape(COEFS, quarter, 128)


VM = pl.BlockSpec(memory_space=pltpu.VMEM)
HB = pl.BlockSpec(memory_space=pltpu.HBM)


def call(kernel, outs, scratch=(), far=()):
    def run(*args):
        args = [pltpu.with_memory_space_constraint(x, pltpu.HBM) if n in far else x for n, x in enumerate(args)]
        return pl.pallas_call(
            kernel,
            out_shape=outs,
            in_specs=[HB if n in far else VM for n in range(len(args))],
            out_specs=jax.tree.map(lambda _: VM, outs),
            scratch_shapes=list(scratch),
            compiler_params=pltpu.CompilerParams(vmem_limit_bytes=20 * 1024 * 1024),
        )(*args)

    return run


def per_device(
    features,
    cotangent,
    w_order0,
    w_order1,
    w_order2,
    w_order3,
    w_order4,
    to_grid,
    from_grid,
    edge_harmonics,
    edge_source,
    edge_target,
    send_list,
):
    rows, atoms = features.shape[2:]
    channels = rows // COEFS
    edges = edge_source.shape[2]
    points = to_grid.shape[0]
    pairs = channels // 16
    like = jax.ShapeDtypeStruct
    same = lambda x: like(x.shape, x.dtype)
    block = like((rows // 4, atoms), BF16)
    grid = like((pairs, points * 8, 2 * atoms), F32)
    *packed, own, lists = call(
        pack_kernel,
        [block] * 8 + [like((rows, atoms), BF16), like(send_list.shape[2:], I32)],
        [pltpu.VMEM((4, rows // 4, 2 * atoms), F32), pltpu.SemaphoreType.DMA((2,))],
        (0, 1),
    )(features[0, 0], send_list[0, 0])
    ghosts = [traded(packed[s], swap) for s, swap in enumerate(SWAPS)]
    kept = (
        cotangent[0, 0],
        w_order0,
        w_order1,
        w_order2,
        w_order3,
        w_order4,
        edge_harmonics[0, 0][:, None, :],
        edge_source[0],
        edge_target[0],
    )
    given = (to_grid.T, from_grid, *kept)
    feat, prod, up, down, fdown, cot, *near = call(
        local_kernel,
        [
            grid,
            grid,
            like((2, points * 8, COEFS * 8), BF16),
            like((2, COEFS * 8, points * 8), BF16),
            like((2, COEFS * 8, points * 8), BF16),
            *map(same, kept),
        ],
        [
            pltpu.VMEM((COEFS, points), F32),
            pltpu.VMEM((COEFS, points), F32),
            pltpu.SemaphoreType.DMA((len(given),)),
        ],
        range(1, 1 + len(given)),
    )(own, *given)
    *weights, harm, src, tgt = near
    results = call(
        edge_kernel,
        [block] * 8 + [grid, grid, like((2, 4, rows // 4, edges), BF16)],
        [
            pltpu.VMEM((COEFS, channels, edges), BF16),
            pltpu.VMEM((rows, 2 * atoms), BF16),
            pltpu.VMEM((rows, atoms), F32),
            pltpu.VMEM((COEFS, channels // 8, 8, atoms), F32),
            pltpu.VMEM((4, rows // 4, 2 * atoms), F32),
        ],
    )(*ghosts, own, src, tgt, harm, *weights, feat, prod, up, down)
    returning = [traded(results[s], swap) for s, swap in enumerate(SWAPS)]
    act, dfeat, dsrc = results[8:]
    layer, grad = call(
        after_kernel,
        [like((COEFS, pairs, 16, atoms), BF16), like((COEFS, channels // 8, 8, atoms), F32)],
    )(own, cot, src, down, fdown, act, dfeat, dsrc)
    total = call(final_kernel, like((COEFS, channels, atoms), F32))(
        *returning, lists, grad.reshape(COEFS, channels, atoms)
    )
    return layer.reshape(1, 1, rows, atoms), total.reshape(1, 1, rows, atoms)


def solution(mesh):
    cell = P("gx", "gy", None, None)
    row = P("gx", "gy", None)
    placed = (cell, cell, P(), P(), P(), P(), P(), P(), P(), cell, row, row, cell)
    return jax.shard_map(
        per_device, mesh=mesh, in_specs=placed, out_specs=(cell, cell), check_vma=False
    )
```

```python
import jax
import jax.numpy as jnp
from jax import lax
from jax.experimental import pallas as pl
from jax.experimental.pallas import tpu as pltpu
from jax.sharding import PartitionSpec as P


F32, BF16, I32 = jnp.float32, jnp.bfloat16, jnp.int32
COEFS = 25
DEGREES = 5
edge_norm = 0.35
SWAPS = ((1, 1), (1, 0), (1, None), (0, 1), (0, 0), (0, None), (None, 1), (None, 0))


def step_of(axis, parity):
    if parity is None:
        return 0
    return jnp.where(lax.rem(lax.axis_index(axis), 2) == parity, 1, -1)


def received_direction(swap):
    place = 3 * (step_of("gx", swap[0]) + 1) + step_of("gy", swap[1]) + 1
    return place - jnp.where(place > 4, 1, 0)


def traded(value, swap):
    nx, ny = lax.axis_size("gx"), lax.axis_size("gy")

    def partner(place, size, parity):
        if parity is None:
            return place
        return (place + (1 if place % 2 == parity else -1)) % size

    pairs = [
        (x * ny + y, partner(x, nx, swap[0]) * ny + partner(y, ny, swap[1]))
        for x in range(nx)
        for y in range(ny)
    ]
    return lax.ppermute(value, ("gx", "gy"), pairs)


def iota(shape, axis):
    return lax.broadcasted_iota(I32, shape, axis)


def dot(a, b):
    return jnp.dot(a, b, preferred_element_type=F32)


def dot_nt(a, b):
    return lax.dot_general(a, b, (((1,), (1,)), ((), ())), preferred_element_type=F32)


def split(value):
    high = value.astype(BF16)
    return high, (value - high.astype(F32)).astype(BF16)


def rows_of(value, part):
    rows, width = value.shape
    quarter = rows // COEFS // 4
    return value.reshape(COEFS, 4, quarter, width)[:, part].reshape(COEFS * quarter, width)


def merged(blocks, part):
    width = blocks[0].shape[1] // 4
    lane = iota((1, 4 * width), 1)
    result = blocks[(3 - part) % 4]
    for m in (2, 1, 0):
        result = jnp.where(lane < (m + 1) * width, blocks[(m - part) % 4], result)
    return result


def lent_lists(lists, atoms):
    place = iota((8, 8), 0)
    wanted = jnp.zeros((8, 8), I32)
    for s, swap in enumerate(SWAPS):
        wanted = jnp.where(place == s, 7 - received_direction(swap), wanted)
    order = (wanted == iota((8, 8), 1)).astype(BF16)
    ghost = lists.shape[1]
    spread = (lax.rem(iota((ghost, atoms), 1), ghost) == iota((ghost, atoms), 0)).astype(BF16)
    chosen = dot(order, lists.astype(F32).astype(BF16)).astype(BF16)
    return dot(chosen, spread).astype(I32)


def lent_pick(lists, q):
    atoms = lists.shape[1]
    row = jnp.concatenate(
        [merged([lists[4 * g + k : 4 * g + k + 1] for k in range(4)], q) for g in range(2)], axis=1
    )
    return (iota((atoms, 2 * atoms), 0) == row).astype(BF16)


def fetch(sources, targets, sems):
    copies = [pltpu.make_async_copy(a, b, sems.at[n]) for n, (a, b) in enumerate(zip(sources, targets))]
    for copy in copies:
        copy.start()
    return copies


def pack_kernel(own_hbm, lists_hbm, *refs):
    outs, own_ref, lists_ref, scratch, sems = refs[:8], refs[8], refs[9], refs[10], refs[11]
    atoms = own_ref.shape[1]
    copies = fetch((lists_hbm, own_hbm), (lists_ref, own_ref), sems)
    copies[0].wait()
    lists = lent_lists(lists_ref[...], atoms)
    picks = [lent_pick(lists, q) for q in range(4)]
    copies[1].wait()
    own = own_ref[...]
    for q in range(4):
        scratch[q] = dot(rows_of(own, q), picks[q])
    for g in range(2):
        for k in range(4):
            parts = [scratch[q, :, atoms * g : atoms * g + atoms] for q in range(4)]
            outs[4 * g + k][...] = merged(parts, k).astype(BF16)


def equal_bits(shape, axis_shift, other_shift):
    return (
        lax.shift_right_logical(iota(shape, 0), axis_shift)
        == lax.shift_right_logical(iota(shape, 1), other_shift)
    ).astype(BF16)


def up_matrices(parts, s):
    points = parts[0].shape[1]
    rows = equal_bits((2 * points, points), 1, 0)
    cols = equal_bits((COEFS, 8 * COEFS), 0, 3)
    wide = [dot(dot_nt(rows, part).astype(BF16), cols) for part in parts]
    row, col = iota(wide[0].shape, 0), iota(wide[0].shape, 1)
    term = lax.bitwise_and(lax.shift_right_logical(col, 1) - s, 3)
    value = jnp.where(term < 2, wide[0], jnp.where(term == 2, wide[1], 0.0))
    return jnp.where(lax.bitwise_and(row, 1) == lax.bitwise_and(col, 1), value, 0.0).astype(BF16)


def down_matrix(part, padded):
    points = part.shape[1]
    shape = (8 * COEFS, 4 * padded)
    row, col = iota(shape, 0), iota(shape, 1)
    slot = sum((col >= m * padded).astype(I32) for m in (1, 2, 3))
    place = iota((points, 4 * padded), 1)
    place = place - padded * sum((place >= m * padded).astype(I32) for m in (1, 2, 3))
    cols = (lax.shift_right_logical(place, 1) == iota((points, 4 * padded), 0)).astype(BF16)
    wide = dot(dot(equal_bits((8 * COEFS, COEFS), 3, 0), part).astype(BF16), cols)
    inner = lax.bitwise_and(col - padded * slot, 1)
    return jnp.where(lax.bitwise_and(row, 7) == 2 * slot + inner, wide, 0.0).astype(BF16)


def channel_pair(value, p):
    width = value.shape[1]
    shaped = value.reshape(COEFS, value.shape[0] // COEFS // 8, 8, width)
    return jnp.concatenate([shaped[:, 2 * p + h] for h in range(2)], axis=2)


def slotted(high, low):
    slot = lax.shift_right_logical(iota((1, 8, 1), 1), 1)
    low = pltpu.roll(low, 2, 1)
    again = pltpu.roll(high, 4, 1)
    width = high.shape[2]
    for s in range(4):
        value = jnp.where(slot == s, high, jnp.where(slot == (s + 1) % 4, low, again))
        yield value.reshape(COEFS * 8, width).astype(BF16)


def filter_rows(columns, harm, filt, q):
    quarter = filt.shape[1] // 4
    scaled = columns.reshape(COEFS, quarter, columns.shape[1]) * harm
    filt[:, q * quarter : (q + 1) * quarter] = scaled.astype(BF16)


def local_kernel(own_ref, *refs):
    given, refs = refs[:11], refs[11:]
    feat_ref, prod_ref, gate_ref, up_ref, down_ref, fdown_ref, part_ref, picks_ref, both_ref = refs[:9]
    turned, kept, refs = refs[9:14], refs[14:23], refs[23:]
    to_ref, from_ref, fup, filt, sems = refs
    copies = fetch(given, (to_ref, from_ref, *kept), sems)
    cot_ref, weights, harm_ref, src_ref, tgt_ref = kept[0], kept[1:6], kept[6], kept[7], kept[8]
    rows, atoms = own_ref.shape
    points = to_ref.shape[1]
    pairs = feat_ref.shape[0]
    padded = feat_ref.shape[1] // 4
    copies[0].wait()
    copies[1].wait()
    to_parts, from_parts = split(to_ref[...]), split(from_ref[...])
    for s in range(4):
        up_ref[s] = up_matrices(to_parts, s)
        fup[s] = up_matrices(from_parts, s)
    for n in range(2):
        down_ref[n] = down_matrix(to_parts[n], padded)
        fdown_ref[n] = down_matrix(from_parts[n], padded)
    for copy in copies[2:]:
        copy.wait()
    own = own_ref[...].astype(F32)
    cot = cot_ref[...].astype(F32)
    for p in range(pairs):
        x = channel_pair(own, p)
        y = channel_pair(cot, p)
        for s, (a, b) in enumerate(zip(slotted(x, jnp.zeros_like(x)), slotted(y, jnp.zeros_like(y)))):
            here = slice(s * padded, s * padded + 2 * points)
            rest = slice(s * padded + 2 * points, (s + 1) * padded)
            feat = dot(up_ref[s], a)
            prod = dot(fup[s], b)
            feat_ref[p, here] = feat
            prod_ref[p, here] = prod
            gate_ref[p, here] = feat * prod
            for ref in (feat_ref, prod_ref):
                ref[p, rest] = jnp.zeros((padded - 2 * points, 2 * atoms), F32)
    src, tgt = src_ref[...], tgt_ref[...]
    edges = src.shape[1]
    ghost = atoms // 4
    target_pick = (iota((atoms, edges), 0) == tgt).astype(BF16)
    both_ref[:atoms] = target_pick
    both_ref[atoms:] = target_pick
    slabs = []
    for swap in SWAPS:
        base = atoms + ghost * received_direction(swap)
        slabs.append((iota((ghost, edges), 0) + base == src).astype(BF16))
    for q in range(4):
        picks_ref[q] = jnp.concatenate(
            [slabs[4 * g + (m - q) % 4] for g in range(2) for m in range(4)], axis=0
        )
    own_pick = (iota((atoms, edges), 0) == src).astype(BF16)
    for q in range(4):
        filter_rows(dot(rows_of(own_ref[...], q), own_pick), harm_ref[...], filt, q)
    part_ref[...] = dot_nt(filt[...].reshape(rows, edges), target_pick)
    turned[0][...] = weights[0][...].T
    for a, b in zip(turned[1:], weights[1:]):
        for n in range(2):
            a[n] = b[n].T


def order_spans(channels):
    spans = []
    offset = DEGREES * channels
    for gap in range(1, DEGREES):
        length = (DEGREES - gap) * channels
        spans.append((offset, offset + length, offset + 2 * length))
        offset += 2 * length
    return spans


def folded(value):
    half = value.shape[1] // 2
    return value[:, :half] + value[:, half:]


def edge_kernel(*refs):
    ghosts, refs = refs[:8], refs[8:]
    weights, turned, refs = refs[:5], refs[5:10], refs[10:]
    picks_ref, both_ref, part_ref, harm_ref, gate_ref, up_ref, down_ref = refs[:7]
    outs, refs = refs[7:15], refs[15:]
    act_ref, dsrc_ref, filt, mixed, agg, dhigh, dlow, dagg, packed = refs
    rows, atoms = part_ref.shape
    channels = rows // COEFS
    edges = both_ref.shape[1]
    pairs = act_ref.shape[0]
    padded = act_ref.shape[1] // 4
    used = up_ref.shape[1]
    blocks = [ghosts[s][...] for s in range(8)]
    for q in range(4):
        taken = jnp.concatenate([merged(blocks[4 * g : 4 * g + 4], q) for g in range(2)], axis=1)
        filter_rows(dot(taken, picks_ref[q]), harm_ref[...], filt, q)
    summed = part_ref[...] + dot_nt(filt[...].reshape(rows, edges), both_ref[:atoms])
    high, low = split(summed)
    mixed[:, :atoms] = high
    mixed[:, atoms:] = low
    zero_rows = DEGREES * channels
    half = 0.5 * edge_norm
    agg[:zero_rows] = folded(dot(weights[0][...], mixed[:zero_rows])) * half
    for w, (begin, mid, end) in zip(weights[1:], order_spans(channels)):
        plus, minus = mixed[begin:mid], mixed[mid:end]
        agg[begin:mid] = folded(dot(w[0], plus) - dot(w[1], minus)) * half
        agg[mid:end] = folded(dot(w[1], plus) + dot(w[0], minus)) * half
    empty = jnp.zeros((padded - used, 2 * atoms), F32)
    for s in range(4):
        rest = slice(s * padded + used, (s + 1) * padded)
        dhigh[rest] = empty.astype(BF16)
        dlow[rest] = empty.astype(BF16)
    for p in range(pairs):
        x = channel_pair(agg[...], p)
        high = x.astype(BF16).astype(F32)
        for s, side in enumerate(slotted(high, x - high)):
            here = slice(s * padded, s * padded + used)
            h = dot(up_ref[s], side)
            t = jnp.tanh(h)
            u = 1.0 + t
            act_ref[p, here] = h * u
            act_ref[p, s * padded + used : (s + 1) * padded] = empty
            a, b = split(gate_ref[p, here] * (u * (1.0 + h * (1.0 - t))))
            dhigh[here] = a
            dlow[here] = b
        down = (dot(down_ref[0], dhigh[...]) + dot(down_ref[0], dlow[...])) * half
        for n in range(2):
            dagg[:, 2 * p + n] = down[:, n * atoms : (n + 1) * atoms].reshape(COEFS, 8, atoms)
    back = dagg[...].reshape(rows, atoms).astype(BF16)

    def keep(begin, end, value):
        high, low = split(value)
        mixed[begin:end, :atoms] = high
        mixed[begin:end, atoms:] = low

    keep(0, zero_rows, dot(turned[0][...], back[:zero_rows]))
    for w, (begin, mid, end) in zip(turned[1:], order_spans(channels)):
        side = jnp.concatenate([back[begin:mid], back[mid:end]], axis=1)
        first, second = dot(w[0], side), dot(w[1], side)
        keep(begin, mid, first[:, :atoms] + second[:, atoms:])
        keep(mid, end, first[:, atoms:] - second[:, :atoms])
    for q in range(4):
        grads = dot(rows_of(mixed[...], q), both_ref[...])
        shaped = grads.reshape(COEFS, grads.shape[0] // COEFS, edges) * harm_ref[...]
        scaled = shaped.reshape(grads.shape).astype(BF16)
        dsrc_ref[q] = scaled
        packed[q] = dot_nt(scaled, picks_ref[q])
    for g in range(2):
        for k in range(4):
            parts = [packed[q, :, atoms * g : atoms * g + atoms] for q in range(4)]
            outs[4 * g + k][...] = merged(parts, k).astype(BF16)


def after_kernel(own_ref, cot_ref, src_ref, down_ref, fdown_ref, act_ref, feat_ref, prod_ref, dsrc_ref, out_ref, grad_ref):
    rows, atoms = own_ref.shape
    channels = rows // COEFS
    edges = src_ref.shape[1]
    own_pick = (iota((atoms, edges), 0) == src_ref[...]).astype(BF16)
    own = own_ref[...].astype(F32).reshape(COEFS, channels // 8, 8, atoms)
    cot = cot_ref[...].astype(F32).reshape(COEFS, channels // 8, 8, atoms)

    def down(parts, value):
        high, low = split(value)
        return dot(parts[0], high) + dot(parts[0], low) + dot(parts[1], high)

    for p in range(channels // 16):
        act = act_ref[p]
        update = down(fdown_ref, act * feat_ref[p])
        grad = down(down_ref, prod_ref[p] * act)
        here = dot_nt(dsrc_ref[p], own_pick).reshape(COEFS, 2, 8, atoms)
        outs = []
        for h in range(2):
            lanes = slice(h * atoms, (h + 1) * atoms)
            outs.append(own[:, 2 * p + h] + update[:, lanes].reshape(COEFS, 8, atoms))
            grad_ref[:, 2 * p + h] = (
                cot[:, 2 * p + h] + grad[:, lanes].reshape(COEFS, 8, atoms) + here[:, h]
            )
        out_ref[:, p] = jnp.concatenate(outs, axis=1).astype(BF16)


def final_kernel(*refs):
    blocks = [r[...] for r in refs[:8]]
    lists_ref, grad_ref, out_hbm, total, sems = refs[8:]
    atoms = grad_ref.shape[2]
    lists = lent_lists(lists_ref[...], atoms)
    copies = []
    for q in range(4):
        taken = jnp.concatenate([merged(blocks[4 * g : 4 * g + 4], q) for g in range(2)], axis=1)
        added = dot_nt(taken, lent_pick(lists, q))
        quarter = added.shape[0] // COEFS
        here = slice(q * quarter, (q + 1) * quarter)
        total[:, here] = grad_ref[:, here] + added.reshape(COEFS, quarter, atoms)
        copies.append(pltpu.make_async_copy(total.at[:, here], out_hbm.at[:, here], sems.at[q]))
        copies[-1].start()
    for copy in copies:
        copy.wait()


VM = pl.BlockSpec(memory_space=pltpu.VMEM)
HB = pl.BlockSpec(memory_space=pltpu.HBM)


def call(kernel, outs, scratch=(), far=(), out_spec=VM):
    def run(*args):
        args = [pltpu.with_memory_space_constraint(x, pltpu.HBM) if n in far else x for n, x in enumerate(args)]
        return pl.pallas_call(
            kernel,
            out_shape=outs,
            in_specs=[HB if n in far else VM for n in range(len(args))],
            out_specs=jax.tree.map(lambda _: out_spec, outs),
            scratch_shapes=list(scratch),
            compiler_params=pltpu.CompilerParams(vmem_limit_bytes=20 * 1024 * 1024),
        )(*args)

    return run


def per_device(
    features,
    cotangent,
    w_order0,
    w_order1,
    w_order2,
    w_order3,
    w_order4,
    to_grid,
    from_grid,
    edge_harmonics,
    edge_source,
    edge_target,
    send_list,
):
    rows, atoms = features.shape[2:]
    channels = rows // COEFS
    edges = edge_source.shape[2]
    points = to_grid.shape[0]
    padded = -(-2 * points // 16) * 16
    pairs = channels // 16
    like = jax.ShapeDtypeStruct
    same = lambda x: like(x.shape, x.dtype)
    block = like((rows // 4, atoms), BF16)
    grid = like((pairs, 4 * padded, 2 * atoms), F32)
    *packed, own, lists = call(
        pack_kernel,
        [block] * 8 + [like((rows, atoms), BF16), like(send_list.shape[2:], I32)],
        [pltpu.VMEM((4, rows // 4, 2 * atoms), F32), pltpu.SemaphoreType.DMA((2,))],
        (0, 1),
    )(features[0, 0], send_list[0, 0])
    ghosts = [traded(packed[s], swap) for s, swap in enumerate(SWAPS)]
    weights = (w_order0, w_order1, w_order2, w_order3, w_order4)
    kept = (
        cotangent[0, 0],
        *weights,
        edge_harmonics[0, 0][:, None, :],
        edge_source[0],
        edge_target[0],
    )
    given = (to_grid.T, from_grid, *kept)
    downs = like((2, 8 * COEFS, 4 * padded), BF16)
    feat, prod, gate, up, down, fdown, part, picks, both, *near = call(
        local_kernel,
        [
            grid,
            grid,
            grid,
            like((4, 2 * points, 8 * COEFS), BF16),
            downs,
            downs,
            like((rows, atoms), F32),
            like((4, 2 * atoms, edges), BF16),
            like((2 * atoms, edges), BF16),
            *map(same, weights),
            *map(same, kept),
        ],
        [
            pltpu.VMEM((COEFS, points), F32),
            pltpu.VMEM((COEFS, points), F32),
            pltpu.VMEM((4, 2 * points, 8 * COEFS), BF16),
            pltpu.VMEM((COEFS, channels, edges), BF16),
            pltpu.SemaphoreType.DMA((len(given),)),
        ],
        range(1, 1 + len(given)),
    )(own, *given)
    turned, (cot, *direct, harm, src, tgt) = near[:5], near[5:]
    *returns, act, dsrc = call(
        edge_kernel,
        [block] * 8 + [grid, like((4, rows // 4, edges), BF16)],
        [
            pltpu.VMEM((COEFS, channels, edges), BF16),
            pltpu.VMEM((rows, 2 * atoms), BF16),
            pltpu.VMEM((rows, atoms), F32),
            pltpu.VMEM((4 * padded, 2 * atoms), BF16),
            pltpu.VMEM((4 * padded, 2 * atoms), BF16),
            pltpu.VMEM((COEFS, channels // 8, 8, atoms), F32),
            pltpu.VMEM((4, rows // 4, 2 * atoms), F32),
        ],
    )(*ghosts, *direct, *turned, picks, both, part, harm, gate, up, down)
    arrived = [traded(returns[s], swap) for s, swap in enumerate(SWAPS)]
    layer, grad = call(
        after_kernel,
        [like((COEFS, pairs, 16, atoms), BF16), like((COEFS, channels // 8, 8, atoms), F32)],
    )(own, cot, src, down, fdown, act, feat, prod, dsrc)
    total = call(
        final_kernel,
        pltpu.HBM((COEFS, channels, atoms), F32),
        [pltpu.VMEM((COEFS, channels, atoms), F32), pltpu.SemaphoreType.DMA((4,))],
        out_spec=HB,
    )(*arrived, lists, grad.reshape(COEFS, channels, atoms))
    return layer.reshape(1, 1, rows, atoms), total.reshape(1, 1, rows, atoms)


def solution(mesh):
    cell = P("gx", "gy", None, None)
    row = P("gx", "gy", None)
    placed = (cell, cell, P(), P(), P(), P(), P(), P(), P(), cell, row, row, cell)
    return jax.shard_map(
        per_device, mesh=mesh, in_specs=placed, out_specs=(cell, cell), check_vma=False
    )
```

```python
import jax
import jax.numpy as jnp
from jax import lax
from jax.experimental import pallas as pl
from jax.experimental.pallas import tpu as pltpu
from jax.sharding import PartitionSpec as P


F32, BF16, I32 = jnp.float32, jnp.bfloat16, jnp.int32
COEFS = 25
DEGREES = 5
edge_norm = 0.35
SWAPS = ((1, None), (0, None), (1, 1), (0, 1), (1, 0), (0, 0), (None, 1), (None, 0))


def step_of(axis, parity):
    if parity is None:
        return 0
    return jnp.where(lax.rem(lax.axis_index(axis), 2) == parity, 1, -1)


def received_direction(swap):
    place = 3 * (step_of("gx", swap[0]) + 1) + step_of("gy", swap[1]) + 1
    return place - jnp.where(place > 4, 1, 0)


def traded(value, swap):
    nx, ny = lax.axis_size("gx"), lax.axis_size("gy")

    def partner(place, size, parity):
        if parity is None:
            return place
        return (place + (1 if place % 2 == parity else -1)) % size

    pairs = [
        (x * ny + y, partner(x, nx, swap[0]) * ny + partner(y, ny, swap[1]))
        for x in range(nx)
        for y in range(ny)
    ]
    return lax.ppermute(value, ("gx", "gy"), pairs)


def iota(shape, axis):
    return lax.broadcasted_iota(I32, shape, axis)


def dot(a, b):
    return jnp.dot(a, b, preferred_element_type=F32)


def dot_nt(a, b):
    return lax.dot_general(a, b, (((1,), (1,)), ((), ())), preferred_element_type=F32)


def split(value):
    high = value.astype(BF16)
    return high, (value - high.astype(F32)).astype(BF16)


def rows_of(value, part):
    rows, width = value.shape
    quarter = rows // COEFS // 4
    return value.reshape(COEFS, 4, quarter, width)[:, part].reshape(COEFS * quarter, width)


def merged(blocks, part):
    width = blocks[0].shape[1] // 4
    lane = iota((1, 4 * width), 1)
    result = blocks[(3 - part) % 4]
    for m in (2, 1, 0):
        result = jnp.where(lane < (m + 1) * width, blocks[(m - part) % 4], result)
    return result


def lent_lists(lists, atoms):
    place = iota((8, 8), 0)
    wanted = jnp.zeros((8, 8), I32)
    for s, swap in enumerate(SWAPS):
        wanted = jnp.where(place == s, 7 - received_direction(swap), wanted)
    order = (wanted == iota((8, 8), 1)).astype(BF16)
    ghost = lists.shape[1]
    spread = (lax.rem(iota((ghost, atoms), 1), ghost) == iota((ghost, atoms), 0)).astype(BF16)
    chosen = dot(order, lists.astype(F32).astype(BF16)).astype(BF16)
    return dot(chosen, spread).astype(I32)


def lent_pick(lists, q, groups):
    atoms = lists.shape[1]
    row = jnp.concatenate(
        [merged([lists[4 * g + k : 4 * g + k + 1] for k in range(4)], q) for g in groups], axis=1
    )
    return (iota((atoms, row.shape[1]), 0) == row).astype(BF16)


def fetch(sources, targets, sems):
    copies = [pltpu.make_async_copy(a, b, sems.at[n]) for n, (a, b) in enumerate(zip(sources, targets))]
    for copy in copies:
        copy.start()
    return copies


def pack_group(own, lists, outs, scratch, g):
    for q in range(4):
        scratch[q] = dot(rows_of(own, q), lent_pick(lists, q, (g,)))
    for k in range(4):
        outs[k][...] = merged([scratch[q] for q in range(4)], k).astype(BF16)


def pack_kernel(own_hbm, lists_hbm, *refs):
    outs, own_ref, lists_ref, scratch, sems = refs[:4], refs[4], refs[5], refs[6], refs[7]
    copies = fetch((lists_hbm, own_hbm), (lists_ref, own_ref), sems)
    copies[0].wait()
    lists = lent_lists(lists_ref[...], own_ref.shape[1])
    copies[1].wait()
    pack_group(own_ref[...], lists, outs, scratch, 0)


def pack_rest_kernel(own_ref, lists_ref, *refs):
    lists = lent_lists(lists_ref[...], own_ref.shape[1])
    pack_group(own_ref[...], lists, refs[:4], refs[4], 1)


def equal_bits(shape, axis_shift, other_shift):
    return (
        lax.shift_right_logical(iota(shape, 0), axis_shift)
        == lax.shift_right_logical(iota(shape, 1), other_shift)
    ).astype(BF16)


def up_matrices(parts, s):
    points = parts[0].shape[1]
    rows = equal_bits((2 * points, points), 1, 0)
    cols = equal_bits((COEFS, 8 * COEFS), 0, 3)
    wide = [dot(dot_nt(rows, part).astype(BF16), cols) for part in parts]
    row, col = iota(wide[0].shape, 0), iota(wide[0].shape, 1)
    term = lax.bitwise_and(lax.shift_right_logical(col, 1) - s, 3)
    value = jnp.where(term < 2, wide[0], jnp.where(term == 2, wide[1], 0.0))
    return jnp.where(lax.bitwise_and(row, 1) == lax.bitwise_and(col, 1), value, 0.0).astype(BF16)


def down_matrix(part, padded):
    points = part.shape[1]
    shape = (8 * COEFS, 4 * padded)
    row, col = iota(shape, 0), iota(shape, 1)
    slot = sum((col >= m * padded).astype(I32) for m in (1, 2, 3))
    place = iota((points, 4 * padded), 1)
    place = place - padded * sum((place >= m * padded).astype(I32) for m in (1, 2, 3))
    cols = (lax.shift_right_logical(place, 1) == iota((points, 4 * padded), 0)).astype(BF16)
    wide = dot(dot(equal_bits((8 * COEFS, COEFS), 3, 0), part).astype(BF16), cols)
    inner = lax.bitwise_and(col - padded * slot, 1)
    return jnp.where(lax.bitwise_and(row, 7) == 2 * slot + inner, wide, 0.0).astype(BF16)


def channel_pair(value, p):
    width = value.shape[1]
    shaped = value.reshape(COEFS, value.shape[0] // COEFS // 8, 8, width)
    return jnp.concatenate([shaped[:, 2 * p + h] for h in range(2)], axis=2)


def slotted(high, low):
    shape = (COEFS * 8, high.shape[2])
    slot = lax.bitwise_and(lax.shift_right_logical(iota((shape[0], 1), 0), 1), 3)
    low = pltpu.roll(low, 2, 1).reshape(shape).astype(BF16)
    again = pltpu.roll(high, 4, 1).reshape(shape).astype(BF16)
    high = high.reshape(shape).astype(BF16)
    for s in range(4):
        yield jnp.where(slot == s, high, jnp.where(slot == (s + 1) % 4, low, again))


def filter_rows(columns, harm, filt, q):
    quarter = filt.shape[1] // 4
    scaled = columns.reshape(COEFS, quarter, columns.shape[1]) * harm
    filt[:, q * quarter : (q + 1) * quarter] = scaled.astype(BF16)


def local_kernel(own_ref, *refs):
    given, refs = refs[:11], refs[11:]
    feat_ref, prod_ref, gate_ref, up_ref, down_ref, fdown_ref, part_ref, picks_ref, both_ref = refs[:9]
    turned, kept, refs = refs[9:14], refs[14:23], refs[23:]
    to_ref, from_ref, fup, filt, sems = refs
    copies = fetch(given, (to_ref, from_ref, *kept), sems)
    cot_ref, weights, harm_ref, src_ref, tgt_ref = kept[0], kept[1:6], kept[6], kept[7], kept[8]
    rows, atoms = own_ref.shape
    points = to_ref.shape[1]
    pairs = feat_ref.shape[0]
    padded = feat_ref.shape[1] // 4
    copies[0].wait()
    copies[1].wait()
    to_parts, from_parts = split(to_ref[...]), split(from_ref[...])
    for s in range(4):
        up_ref[s] = up_matrices(to_parts, s)
        fup[s] = up_matrices(from_parts, s)
    for n in range(2):
        down_ref[n] = down_matrix(to_parts[n], padded)
        fdown_ref[n] = down_matrix(from_parts[n], padded)
    for copy in copies[2:]:
        copy.wait()
    own = own_ref[...].astype(F32)
    cot = cot_ref[...].astype(F32)
    for p in range(pairs):
        x = channel_pair(own, p)
        y = channel_pair(cot, p)
        for s, (a, b) in enumerate(zip(slotted(x, jnp.zeros_like(x)), slotted(y, jnp.zeros_like(y)))):
            here = slice(s * padded, s * padded + 2 * points)
            rest = slice(s * padded + 2 * points, (s + 1) * padded)
            feat = dot(up_ref[s], a)
            prod = dot(fup[s], b)
            feat_ref[p, here] = feat
            prod_ref[p, here] = prod
            gate_ref[p, here] = feat * prod
            for ref in (feat_ref, prod_ref):
                ref[p, rest] = jnp.zeros((padded - 2 * points, 2 * atoms), F32)
    src, tgt = src_ref[...], tgt_ref[...]
    edges = src.shape[1]
    ghost = atoms // 4
    target_pick = (iota((atoms, edges), 0) == tgt).astype(BF16)
    both_ref[:atoms] = target_pick
    both_ref[atoms:] = target_pick
    slabs = []
    for swap in SWAPS:
        base = atoms + ghost * received_direction(swap)
        slabs.append((iota((ghost, edges), 0) + base == src).astype(BF16))
    for q in range(4):
        picks_ref[q] = jnp.concatenate(
            [slabs[4 * g + (m - q) % 4] for g in range(2) for m in range(4)], axis=0
        )
    own_pick = (iota((atoms, edges), 0) == src).astype(BF16)
    for q in range(4):
        filter_rows(dot(rows_of(own_ref[...], q), own_pick), harm_ref[...], filt, q)
    part_ref[...] = dot_nt(filt[...].reshape(rows, edges), target_pick)
    turned[0][...] = weights[0][...].T
    for a, b in zip(turned[1:], weights[1:]):
        for n in range(2):
            a[n] = b[n].T


def order_spans(channels):
    spans = []
    offset = DEGREES * channels
    for gap in range(1, DEGREES):
        length = (DEGREES - gap) * channels
        spans.append((offset, offset + length, offset + 2 * length))
        offset += 2 * length
    return spans


def folded(value):
    half = value.shape[1] // 2
    return value[:, :half] + value[:, half:]


def edge_kernel(*refs):
    ghosts, refs = refs[:8], refs[8:]
    weights, turned, refs = refs[:5], refs[5:10], refs[10:]
    picks_ref, both_ref, part_ref, harm_ref, gate_ref, up_ref, down_ref = refs[:7]
    outs, refs = refs[7:11], refs[11:]
    act_ref, dsrc_ref, filt, mixed, agg, dgrid, dagg, packed = refs
    rows, atoms = part_ref.shape
    channels = rows // COEFS
    edges = both_ref.shape[1]
    pairs = act_ref.shape[0]
    padded = act_ref.shape[1] // 4
    used = up_ref.shape[1]
    blocks = [ghosts[s][...] for s in range(8)]
    for q in range(4):
        taken = jnp.concatenate([merged(blocks[4 * g : 4 * g + 4], q) for g in range(2)], axis=1)
        filter_rows(dot(taken, picks_ref[q]), harm_ref[...], filt, q)
    summed = part_ref[...] + dot_nt(filt[...].reshape(rows, edges), both_ref[:atoms])
    high, low = split(summed)
    mixed[:, :atoms] = high
    mixed[:, atoms:] = low
    zero_rows = DEGREES * channels
    half = 0.5 * edge_norm
    agg[:zero_rows] = folded(dot(weights[0][...], mixed[:zero_rows])) * half
    for w, (begin, mid, end) in zip(weights[1:], order_spans(channels)):
        plus, minus = mixed[begin:mid], mixed[mid:end]
        agg[begin:mid] = folded(dot(w[0], plus) - dot(w[1], minus)) * half
        agg[mid:end] = folded(dot(w[1], plus) + dot(w[0], minus)) * half
    empty = jnp.zeros((padded - used, 2 * atoms), F32)
    for s in range(4):
        rest = slice(s * padded + used, (s + 1) * padded)
        dgrid[rest] = empty.astype(BF16)
    for p in range(pairs):
        x = channel_pair(agg[...], p)
        high = x.astype(BF16).astype(F32)
        for s, side in enumerate(slotted(high, x - high)):
            here = slice(s * padded, s * padded + used)
            h = dot(up_ref[s], side)
            t = jnp.tanh(h)
            u = 1.0 + t
            act = h * u
            act_ref[p, here] = act
            act_ref[p, s * padded + used : (s + 1) * padded] = empty
            dgrid[here] = (gate_ref[p, here] * (u + act * (1.0 - t))).astype(BF16)
        down = dot(down_ref[0], dgrid[...]) * half
        for n in range(2):
            dagg[:, 2 * p + n] = down[:, n * atoms : (n + 1) * atoms].reshape(COEFS, 8, atoms)
    back = dagg[...].reshape(rows, atoms).astype(BF16)

    def keep(begin, end, value):
        high, low = split(value)
        mixed[begin:end, :atoms] = high
        mixed[begin:end, atoms:] = low

    keep(0, zero_rows, dot(turned[0][...], back[:zero_rows]))
    for w, (begin, mid, end) in zip(turned[1:], order_spans(channels)):
        side = jnp.concatenate([back[begin:mid], back[mid:end]], axis=1)
        first, second = dot(w[0], side), dot(w[1], side)
        keep(begin, mid, first[:, :atoms] + second[:, atoms:])
        keep(mid, end, first[:, atoms:] - second[:, :atoms])
    for q in range(4):
        grads = dot(rows_of(mixed[...], q), both_ref[...])
        shaped = grads.reshape(COEFS, grads.shape[0] // COEFS, edges) * harm_ref[...]
        scaled = shaped.reshape(grads.shape).astype(BF16)
        dsrc_ref[q] = scaled
    return_group(dsrc_ref, picks_ref, outs, packed, 0)


def return_group(dsrc_ref, picks_ref, outs, packed, g):
    half = picks_ref.shape[1] // 2
    for q in range(4):
        packed[q] = dot_nt(dsrc_ref[q], picks_ref[q, g * half : (g + 1) * half]).astype(BF16)
    for k in range(4):
        outs[k][...] = merged([packed[q] for q in range(4)], k)


def edge_rest_kernel(dsrc_ref, picks_ref, *refs):
    return_group(dsrc_ref, picks_ref, refs[:4], refs[4], 1)


def after_kernel(own_ref, cot_ref, src_ref, down_ref, fdown_ref, act_ref, feat_ref, prod_ref, dsrc_ref, out_ref, grad_ref):
    rows, atoms = own_ref.shape
    channels = rows // COEFS
    edges = src_ref.shape[1]
    own_pick = (iota((atoms, edges), 0) == src_ref[...]).astype(BF16)
    own = own_ref[...].astype(F32).reshape(COEFS, channels // 8, 8, atoms)
    cot = cot_ref[...].astype(F32).reshape(COEFS, channels // 8, 8, atoms)

    def down(parts, value):
        high, low = split(value)
        return dot(parts[0], high) + dot(parts[0], low) + dot(parts[1], high)

    for p in range(channels // 16):
        act = act_ref[p]
        update = down(fdown_ref, act * feat_ref[p])
        grad = down(down_ref, prod_ref[p] * act)
        here = dot_nt(dsrc_ref[p], own_pick).reshape(COEFS, 2, 8, atoms)
        outs = []
        for h in range(2):
            lanes = slice(h * atoms, (h + 1) * atoms)
            outs.append(own[:, 2 * p + h] + update[:, lanes].reshape(COEFS, 8, atoms))
            grad_ref[:, 2 * p + h] = (
                cot[:, 2 * p + h] + grad[:, lanes].reshape(COEFS, 8, atoms) + here[:, h]
            )
        out_ref[:, p] = jnp.concatenate(outs, axis=1).astype(BF16)


def final_kernel(*refs):
    blocks = [r[...] for r in refs[:8]]
    lists_ref, grad_ref, out_hbm, total, sems = refs[8:]
    atoms = grad_ref.shape[2]
    lists = lent_lists(lists_ref[...], atoms)
    copies = []
    for q in range(4):
        taken = jnp.concatenate([merged(blocks[4 * g : 4 * g + 4], q) for g in range(2)], axis=1)
        added = dot_nt(taken, lent_pick(lists, q, (0, 1)))
        quarter = added.shape[0] // COEFS
        here = slice(q * quarter, (q + 1) * quarter)
        total[:, here] = grad_ref[:, here] + added.reshape(COEFS, quarter, atoms)
        copies.append(pltpu.make_async_copy(total.at[:, here], out_hbm.at[:, here], sems.at[q]))
        copies[-1].start()
    for copy in copies:
        copy.wait()


VM = pl.BlockSpec(memory_space=pltpu.VMEM)
HB = pl.BlockSpec(memory_space=pltpu.HBM)


def call(kernel, outs, scratch=(), far=(), out_spec=VM):
    def run(*args):
        args = [pltpu.with_memory_space_constraint(x, pltpu.HBM) if n in far else x for n, x in enumerate(args)]
        return pl.pallas_call(
            kernel,
            out_shape=outs,
            in_specs=[HB if n in far else VM for n in range(len(args))],
            out_specs=jax.tree.map(lambda _: out_spec, outs),
            scratch_shapes=list(scratch),
            compiler_params=pltpu.CompilerParams(vmem_limit_bytes=20 * 1024 * 1024),
        )(*args)

    return run


def per_device(
    features,
    cotangent,
    w_order0,
    w_order1,
    w_order2,
    w_order3,
    w_order4,
    to_grid,
    from_grid,
    edge_harmonics,
    edge_source,
    edge_target,
    send_list,
):
    rows, atoms = features.shape[2:]
    channels = rows // COEFS
    edges = edge_source.shape[2]
    points = to_grid.shape[0]
    padded = -(-2 * points // 16) * 16
    pairs = channels // 16
    like = jax.ShapeDtypeStruct
    same = lambda x: like(x.shape, x.dtype)
    block = like((rows // 4, atoms), BF16)
    grid = like((pairs, 4 * padded, 2 * atoms), F32)
    *packed, own, lists = call(
        pack_kernel,
        [block] * 4 + [like((rows, atoms), BF16), like(send_list.shape[2:], I32)],
        [pltpu.VMEM((4, rows // 4, atoms), F32), pltpu.SemaphoreType.DMA((2,))],
        (0, 1),
    )(features[0, 0], send_list[0, 0])
    packed += call(pack_rest_kernel, [block] * 4, [pltpu.VMEM((4, rows // 4, atoms), F32)])(own, lists)
    ghosts = [traded(packed[s], swap) for s, swap in enumerate(SWAPS)]
    weights = (w_order0, w_order1, w_order2, w_order3, w_order4)
    kept = (
        cotangent[0, 0],
        *weights,
        edge_harmonics[0, 0][:, None, :],
        edge_source[0],
        edge_target[0],
    )
    given = (to_grid.T, from_grid, *kept)
    downs = like((2, 8 * COEFS, 4 * padded), BF16)
    feat, prod, gate, up, down, fdown, part, picks, both, *near = call(
        local_kernel,
        [
            grid,
            grid,
            grid,
            like((4, 2 * points, 8 * COEFS), BF16),
            downs,
            downs,
            like((rows, atoms), F32),
            like((4, 2 * atoms, edges), BF16),
            like((2 * atoms, edges), BF16),
            *map(same, weights),
            *map(same, kept),
        ],
        [
            pltpu.VMEM((COEFS, points), F32),
            pltpu.VMEM((COEFS, points), F32),
            pltpu.VMEM((4, 2 * points, 8 * COEFS), BF16),
            pltpu.VMEM((COEFS, channels, edges), BF16),
            pltpu.SemaphoreType.DMA((len(given),)),
        ],
        range(1, 1 + len(given)),
    )(own, *given)
    turned, (cot, *direct, harm, src, tgt) = near[:5], near[5:]
    *returns, act, dsrc = call(
        edge_kernel,
        [block] * 4 + [grid, like((4, rows // 4, edges), BF16)],
        [
            pltpu.VMEM((COEFS, channels, edges), BF16),
            pltpu.VMEM((rows, 2 * atoms), BF16),
            pltpu.VMEM((rows, atoms), F32),
            pltpu.VMEM((4 * padded, 2 * atoms), BF16),
            pltpu.VMEM((COEFS, channels // 8, 8, atoms), F32),
            pltpu.VMEM((4, rows // 4, atoms), BF16),
        ],
    )(*ghosts, *direct, *turned, picks, both, part, harm, gate, up, down)
    returns += call(edge_rest_kernel, [block] * 4, [pltpu.VMEM((4, rows // 4, atoms), BF16)])(dsrc, picks)
    arrived = [traded(returns[s], swap) for s, swap in enumerate(SWAPS)]
    layer, grad = call(
        after_kernel,
        [like((COEFS, pairs, 16, atoms), BF16), like((COEFS, channels // 8, 8, atoms), F32)],
    )(own, cot, src, down, fdown, act, feat, prod, dsrc)
    total = call(
        final_kernel,
        pltpu.HBM((COEFS, channels, atoms), F32),
        [pltpu.VMEM((COEFS, channels, atoms), F32), pltpu.SemaphoreType.DMA((4,))],
        out_spec=HB,
    )(*arrived, lists, grad.reshape(COEFS, channels, atoms))
    return layer.reshape(1, 1, rows, atoms), total.reshape(1, 1, rows, atoms)


def solution(mesh):
    cell = P("gx", "gy", None, None)
    row = P("gx", "gy", None)
    placed = (cell, cell, P(), P(), P(), P(), P(), P(), P(), cell, row, row, cell)
    return jax.shard_map(
        per_device, mesh=mesh, in_specs=placed, out_specs=(cell, cell), check_vma=False
    )
```

```python
import jax
import jax.numpy as jnp
from jax import lax
from jax.experimental import pallas as pl
from jax.experimental.pallas import tpu as pltpu
from jax.sharding import PartitionSpec as P


F32, BF16, I32 = jnp.float32, jnp.bfloat16, jnp.int32
COEFS = 25
DEGREES = 5
edge_norm = 0.35
SWAPS = ((0, None), (1, None), (1, 1), (0, 1), (1, 0), (0, 0), (None, 1), (None, 0))


def step_of(axis, parity):
    if parity is None:
        return 0
    return jnp.where(lax.rem(lax.axis_index(axis), 2) == parity, 1, -1)


def received_direction(swap):
    place = 3 * (step_of("gx", swap[0]) + 1) + step_of("gy", swap[1]) + 1
    return place - jnp.where(place > 4, 1, 0)


def traded(value, swap):
    nx, ny = lax.axis_size("gx"), lax.axis_size("gy")

    def partner(place, size, parity):
        if parity is None:
            return place
        return (place + (1 if place % 2 == parity else -1)) % size

    pairs = [
        (x * ny + y, partner(x, nx, swap[0]) * ny + partner(y, ny, swap[1]))
        for x in range(nx)
        for y in range(ny)
    ]
    return lax.ppermute(value, ("gx", "gy"), pairs)


def iota(shape, axis):
    return lax.broadcasted_iota(I32, shape, axis)


def dot(a, b):
    return jnp.dot(a, b, preferred_element_type=F32)


def dot_nt(a, b):
    return lax.dot_general(a, b, (((1,), (1,)), ((), ())), preferred_element_type=F32)


def split(value):
    high = value.astype(BF16)
    return high, (value - high.astype(F32)).astype(BF16)


def rows_of(value, part):
    rows, width = value.shape
    quarter = rows // COEFS // 4
    return value.reshape(COEFS, 4, quarter, width)[:, part].reshape(COEFS * quarter, width)


def merged(blocks, part):
    width = blocks[0].shape[1] // 4
    lane = iota((1, 4 * width), 1)
    result = blocks[(3 - part) % 4]
    for m in (2, 1, 0):
        result = jnp.where(lane < (m + 1) * width, blocks[(m - part) % 4], result)
    return result


def lent_lists(lists_ref, swaps):
    rows = [lists_ref[pl.ds(7 - received_direction(swap), 1), :] for swap in swaps]
    return [jnp.concatenate([row] * 4, axis=1) for row in rows]


def lent_pick(lists, q):
    row = merged(lists, q)
    return (iota((row.shape[1], row.shape[1]), 0) == row).astype(BF16)


def fetch(sources, targets, sems):
    copies = [pltpu.make_async_copy(a, b, sems.at[n]) for n, (a, b) in enumerate(zip(sources, targets))]
    for copy in copies:
        copy.start()
    return copies


def pack_group(own, lists, outs, scratch):
    for q in range(4):
        scratch[q] = dot(rows_of(own, q), lent_pick(lists, q))
    for k in range(4):
        outs[k][...] = merged([scratch[q] for q in range(4)], k).astype(BF16)


def pack_kernel(own_hbm, lists_hbm, *refs):
    outs, own_ref, lists_ref, scratch, sems = refs[:4], refs[4], refs[5], refs[6], refs[7]
    copies = fetch((lists_hbm, own_hbm), (lists_ref, own_ref), sems)
    copies[0].wait()
    lists = lent_lists(lists_ref, SWAPS[:4])
    copies[1].wait()
    pack_group(own_ref[...], lists, outs, scratch)


def pack_rest_kernel(own_ref, lists_ref, *refs):
    pack_group(own_ref[...], lent_lists(lists_ref, SWAPS[4:]), refs[:4], refs[4])


def equal_bits(shape, axis_shift, other_shift):
    return (
        lax.shift_right_logical(iota(shape, 0), axis_shift)
        == lax.shift_right_logical(iota(shape, 1), other_shift)
    ).astype(BF16)


def up_matrices(parts, s):
    points = parts[0].shape[1]
    rows = equal_bits((2 * points, points), 1, 0)
    cols = equal_bits((COEFS, 8 * COEFS), 0, 3)
    wide = [dot(dot_nt(rows, part).astype(BF16), cols) for part in parts]
    row, col = iota(wide[0].shape, 0), iota(wide[0].shape, 1)
    term = lax.bitwise_and(lax.shift_right_logical(col, 1) - s, 3)
    value = jnp.where(term < 2, wide[0], jnp.where(term == 2, wide[1], 0.0))
    return jnp.where(lax.bitwise_and(row, 1) == lax.bitwise_and(col, 1), value, 0.0).astype(BF16)


def down_matrix(part, padded):
    points = part.shape[1]
    shape = (8 * COEFS, 4 * padded)
    row, col = iota(shape, 0), iota(shape, 1)
    slot = sum((col >= m * padded).astype(I32) for m in (1, 2, 3))
    place = iota((points, 4 * padded), 1)
    place = place - padded * sum((place >= m * padded).astype(I32) for m in (1, 2, 3))
    cols = (lax.shift_right_logical(place, 1) == iota((points, 4 * padded), 0)).astype(BF16)
    wide = dot(dot(equal_bits((8 * COEFS, COEFS), 3, 0), part).astype(BF16), cols)
    inner = lax.bitwise_and(col - padded * slot, 1)
    return jnp.where(lax.bitwise_and(row, 7) == 2 * slot + inner, wide, 0.0).astype(BF16)


def channel_pair(value, p):
    width = value.shape[1]
    shaped = value.reshape(COEFS, value.shape[0] // COEFS // 8, 8, width)
    return jnp.concatenate([shaped[:, 2 * p + h] for h in range(2)], axis=2)


def slotted(high, low):
    shape = (COEFS * 8, high.shape[2])
    slot = lax.bitwise_and(lax.shift_right_logical(iota((shape[0], 1), 0), 1), 3)
    low = pltpu.roll(low, 2, 1).reshape(shape).astype(BF16)
    again = pltpu.roll(high, 4, 1).reshape(shape).astype(BF16)
    high = high.reshape(shape).astype(BF16)
    for s in range(4):
        yield jnp.where(slot == s, high, jnp.where(slot == (s + 1) % 4, low, again))


def filter_rows(columns, harm, filt, q):
    quarter = filt.shape[1] // 4
    scaled = columns.reshape(COEFS, quarter, columns.shape[1]) * harm
    filt[:, q * quarter : (q + 1) * quarter] = scaled.astype(BF16)


def local_kernel(own_ref, *refs):
    given, refs = refs[:11], refs[11:]
    feat_ref, prod_ref, gate_ref, up_ref, down_ref, fdown_ref, part_ref, picks_ref, both_ref = refs[:9]
    turned, kept, refs = refs[9:14], refs[14:23], refs[23:]
    to_ref, from_ref, fup, filt, sems = refs
    copies = fetch(given, (to_ref, from_ref, *kept), sems)
    cot_ref, weights, harm_ref, src_ref, tgt_ref = kept[0], kept[1:6], kept[6], kept[7], kept[8]
    rows, atoms = own_ref.shape
    points = to_ref.shape[1]
    pairs = feat_ref.shape[0]
    padded = feat_ref.shape[1] // 4
    copies[0].wait()
    copies[1].wait()
    to_parts, from_parts = split(to_ref[...]), split(from_ref[...])
    for s in range(4):
        up_ref[s] = up_matrices(to_parts, s)
        fup[s] = up_matrices(from_parts, s)
    for n in range(2):
        down_ref[n] = down_matrix(to_parts[n], padded)
        fdown_ref[n] = down_matrix(from_parts[n], padded)
    for copy in copies[2:]:
        copy.wait()
    own = own_ref[...].astype(F32)
    cot = cot_ref[...].astype(F32)
    for p in range(pairs):
        x = channel_pair(own, p)
        y = channel_pair(cot, p)
        for s, (a, b) in enumerate(zip(slotted(x, jnp.zeros_like(x)), slotted(y, jnp.zeros_like(y)))):
            here = slice(s * padded, s * padded + 2 * points)
            rest = slice(s * padded + 2 * points, (s + 1) * padded)
            feat = dot(up_ref[s], a)
            prod = dot(fup[s], b)
            feat_ref[p, here] = feat
            prod_ref[p, here] = prod
            gate_ref[p, here] = feat * prod
            for ref in (feat_ref, prod_ref):
                ref[p, rest] = jnp.zeros((padded - 2 * points, 2 * atoms), F32)
    src, tgt = src_ref[...], tgt_ref[...]
    edges = src.shape[1]
    ghost = atoms // 4
    target_pick = (iota((atoms, edges), 0) == tgt).astype(BF16)
    both_ref[:atoms] = target_pick
    both_ref[atoms:] = target_pick
    slabs = []
    for swap in SWAPS:
        base = atoms + ghost * received_direction(swap)
        slabs.append((iota((ghost, edges), 0) + base == src).astype(BF16))
    for q in range(4):
        picks_ref[q] = jnp.concatenate(
            [slabs[4 * g + (m - q) % 4] for g in range(2) for m in range(4)], axis=0
        )
    own_pick = (iota((atoms, edges), 0) == src).astype(BF16)
    for q in range(4):
        filter_rows(dot(rows_of(own_ref[...], q), own_pick), harm_ref[...], filt, q)
    part_ref[...] = dot_nt(filt[...].reshape(rows, edges), target_pick)
    turned[0][...] = weights[0][...].T
    for a, b in zip(turned[1:], weights[1:]):
        for n in range(2):
            a[n] = b[n].T


def order_spans(channels):
    spans = []
    offset = DEGREES * channels
    for gap in range(1, DEGREES):
        length = (DEGREES - gap) * channels
        spans.append((offset, offset + length, offset + 2 * length))
        offset += 2 * length
    return spans


def folded(value):
    half = value.shape[1] // 2
    return value[:, :half] + value[:, half:]


def edge_kernel(*refs):
    ghosts, refs = refs[:8], refs[8:]
    weights, turned, refs = refs[:5], refs[5:10], refs[10:]
    picks_ref, both_ref, part_ref, harm_ref, gate_ref, up_ref, down_ref = refs[:7]
    outs, refs = refs[7:11], refs[11:]
    act_ref, dsrc_ref, filt, mixed, agg, dgrid, dagg, packed = refs
    rows, atoms = part_ref.shape
    channels = rows // COEFS
    edges = both_ref.shape[1]
    pairs = act_ref.shape[0]
    padded = act_ref.shape[1] // 4
    used = up_ref.shape[1]
    blocks = [ghosts[s][...] for s in range(8)]
    for q in range(4):
        taken = jnp.concatenate([merged(blocks[4 * g : 4 * g + 4], q) for g in range(2)], axis=1)
        filter_rows(dot(taken, picks_ref[q]), harm_ref[...], filt, q)
    summed = part_ref[...] + dot_nt(filt[...].reshape(rows, edges), both_ref[:atoms])
    high, low = split(summed)
    mixed[:, :atoms] = high
    mixed[:, atoms:] = low
    zero_rows = DEGREES * channels
    half = 0.5 * edge_norm
    agg[:zero_rows] = folded(dot(weights[0][...], mixed[:zero_rows])) * half
    for w, (begin, mid, end) in zip(weights[1:], order_spans(channels)):
        plus, minus = mixed[begin:mid], mixed[mid:end]
        agg[begin:mid] = folded(dot(w[0], plus) - dot(w[1], minus)) * half
        agg[mid:end] = folded(dot(w[1], plus) + dot(w[0], minus)) * half
    empty = jnp.zeros((padded - used, 2 * atoms), F32)
    for s in range(4):
        rest = slice(s * padded + used, (s + 1) * padded)
        dgrid[rest] = empty.astype(BF16)
    for p in range(pairs):
        x = channel_pair(agg[...], p)
        high = x.astype(BF16).astype(F32)
        for s, side in enumerate(slotted(high, x - high)):
            here = slice(s * padded, s * padded + used)
            h = dot(up_ref[s], side)
            t = jnp.tanh(h)
            u = 1.0 + t
            act = h * u
            act_ref[p, here] = act
            act_ref[p, s * padded + used : (s + 1) * padded] = empty
            dgrid[here] = (gate_ref[p, here] * (u + act * (1.0 - t))).astype(BF16)
        down = dot(down_ref[0], dgrid[...]) * half
        for n in range(2):
            dagg[:, 2 * p + n] = down[:, n * atoms : (n + 1) * atoms].reshape(COEFS, 8, atoms)
    back = dagg[...].reshape(rows, atoms).astype(BF16)

    def keep(begin, end, value):
        high, low = split(value)
        mixed[begin:end, :atoms] = high
        mixed[begin:end, atoms:] = low

    keep(0, zero_rows, dot(turned[0][...], back[:zero_rows]))
    for w, (begin, mid, end) in zip(turned[1:], order_spans(channels)):
        side = jnp.concatenate([back[begin:mid], back[mid:end]], axis=1)
        first, second = dot(w[0], side), dot(w[1], side)
        keep(begin, mid, first[:, :atoms] + second[:, atoms:])
        keep(mid, end, first[:, atoms:] - second[:, :atoms])
    for q in range(4):
        grads = dot(rows_of(mixed[...], q), both_ref[...])
        shaped = grads.reshape(COEFS, grads.shape[0] // COEFS, edges) * harm_ref[...]
        scaled = shaped.reshape(grads.shape).astype(BF16)
        dsrc_ref[q] = scaled
    return_group(dsrc_ref, picks_ref, outs, packed, 0)


def return_group(dsrc_ref, picks_ref, outs, packed, g):
    half = picks_ref.shape[1] // 2
    for q in range(4):
        packed[q] = dot_nt(dsrc_ref[q], picks_ref[q, g * half : (g + 1) * half]).astype(BF16)
    for k in range(4):
        outs[k][...] = merged([packed[q] for q in range(4)], k)


def edge_rest_kernel(dsrc_ref, picks_ref, *refs):
    return_group(dsrc_ref, picks_ref, refs[:4], refs[4], 1)


def after_kernel(*refs):
    own_ref, cot_ref, src_ref, lists_ref, down_ref, fdown_ref = refs[:6]
    act_ref, feat_ref, prod_ref, dsrc_ref, out_ref, grad_ref, lent_ref = refs[6:]
    rows, atoms = own_ref.shape
    channels = rows // COEFS
    edges = src_ref.shape[1]
    own_pick = (iota((atoms, edges), 0) == src_ref[...]).astype(BF16)
    own = own_ref[...].astype(F32).reshape(COEFS, channels // 8, 8, atoms)
    cot = cot_ref[...].astype(F32).reshape(COEFS, channels // 8, 8, atoms)

    for g in range(2):
        lists = lent_lists(lists_ref, SWAPS[4 * g : 4 * g + 4])
        for q in range(4):
            lent_ref[q, :, g * atoms : (g + 1) * atoms] = lent_pick(lists, q)

    def down(parts, value):
        high, low = split(value)
        return dot(parts[0], high) + dot(parts[0], low) + dot(parts[1], high)

    for p in range(channels // 16):
        act = act_ref[p]
        update = down(fdown_ref, act * feat_ref[p])
        grad = down(down_ref, prod_ref[p] * act)
        here = dot_nt(dsrc_ref[p], own_pick).reshape(COEFS, 2, 8, atoms)
        outs = []
        for h in range(2):
            lanes = slice(h * atoms, (h + 1) * atoms)
            outs.append(own[:, 2 * p + h] + update[:, lanes].reshape(COEFS, 8, atoms))
            grad_ref[:, 2 * p + h] = (
                cot[:, 2 * p + h] + grad[:, lanes].reshape(COEFS, 8, atoms) + here[:, h]
            )
        out_ref[:, p] = jnp.concatenate(outs, axis=1).astype(BF16)


def final_kernel(*refs):
    blocks = [r[...] for r in refs[:8]]
    lent_ref, grad_ref, out_hbm, total, sems = refs[8:]
    atoms = grad_ref.shape[2]
    copies = []
    for q in range(4):
        taken = jnp.concatenate([merged(blocks[4 * g : 4 * g + 4], q) for g in range(2)], axis=1)
        added = dot_nt(taken, lent_ref[q])
        quarter = added.shape[0] // COEFS
        here = slice(q * quarter, (q + 1) * quarter)
        total[:, here] = grad_ref[:, here] + added.reshape(COEFS, quarter, atoms)
        copies.append(pltpu.make_async_copy(total.at[:, here], out_hbm.at[:, here], sems.at[q]))
        copies[-1].start()
    for copy in copies:
        copy.wait()


VM = pl.BlockSpec(memory_space=pltpu.VMEM)
HB = pl.BlockSpec(memory_space=pltpu.HBM)


def call(kernel, outs, scratch=(), far=(), out_spec=VM):
    def run(*args):
        args = [pltpu.with_memory_space_constraint(x, pltpu.HBM) if n in far else x for n, x in enumerate(args)]
        return pl.pallas_call(
            kernel,
            out_shape=outs,
            in_specs=[HB if n in far else VM for n in range(len(args))],
            out_specs=jax.tree.map(lambda _: out_spec, outs),
            scratch_shapes=list(scratch),
            compiler_params=pltpu.CompilerParams(vmem_limit_bytes=20 * 1024 * 1024),
        )(*args)

    return run


def per_device(
    features,
    cotangent,
    w_order0,
    w_order1,
    w_order2,
    w_order3,
    w_order4,
    to_grid,
    from_grid,
    edge_harmonics,
    edge_source,
    edge_target,
    send_list,
):
    rows, atoms = features.shape[2:]
    channels = rows // COEFS
    edges = edge_source.shape[2]
    points = to_grid.shape[0]
    padded = -(-2 * points // 16) * 16
    pairs = channels // 16
    like = jax.ShapeDtypeStruct
    same = lambda x: like(x.shape, x.dtype)
    block = like((rows // 4, atoms), BF16)
    grid = like((pairs, 4 * padded, 2 * atoms), F32)
    *packed, own, lists = call(
        pack_kernel,
        [block] * 4 + [like((rows, atoms), BF16), like(send_list.shape[2:], I32)],
        [pltpu.VMEM((4, rows // 4, atoms), F32), pltpu.SemaphoreType.DMA((2,))],
        (0, 1),
    )(features[0, 0], send_list[0, 0])
    packed += call(pack_rest_kernel, [block] * 4, [pltpu.VMEM((4, rows // 4, atoms), F32)])(own, lists)
    ghosts = [traded(packed[s], swap) for s, swap in enumerate(SWAPS)]
    weights = (w_order0, w_order1, w_order2, w_order3, w_order4)
    kept = (
        cotangent[0, 0],
        *weights,
        edge_harmonics[0, 0][:, None, :],
        edge_source[0],
        edge_target[0],
    )
    given = (to_grid.T, from_grid, *kept)
    downs = like((2, 8 * COEFS, 4 * padded), BF16)
    feat, prod, gate, up, down, fdown, part, picks, both, *near = call(
        local_kernel,
        [
            grid,
            grid,
            grid,
            like((4, 2 * points, 8 * COEFS), BF16),
            downs,
            downs,
            like((rows, atoms), F32),
            like((4, 2 * atoms, edges), BF16),
            like((2 * atoms, edges), BF16),
            *map(same, weights),
            *map(same, kept),
        ],
        [
            pltpu.VMEM((COEFS, points), F32),
            pltpu.VMEM((COEFS, points), F32),
            pltpu.VMEM((4, 2 * points, 8 * COEFS), BF16),
            pltpu.VMEM((COEFS, channels, edges), BF16),
            pltpu.SemaphoreType.DMA((len(given),)),
        ],
        range(1, 1 + len(given)),
    )(own, *given)
    turned, (cot, *direct, harm, src, tgt) = near[:5], near[5:]
    *returns, act, dsrc = call(
        edge_kernel,
        [block] * 4 + [grid, like((4, rows // 4, edges), BF16)],
        [
            pltpu.VMEM((COEFS, channels, edges), BF16),
            pltpu.VMEM((rows, 2 * atoms), BF16),
            pltpu.VMEM((rows, atoms), F32),
            pltpu.VMEM((4 * padded, 2 * atoms), BF16),
            pltpu.VMEM((COEFS, channels // 8, 8, atoms), F32),
            pltpu.VMEM((4, rows // 4, atoms), BF16),
        ],
    )(*ghosts, *direct, *turned, picks, both, part, harm, gate, up, down)
    returns += call(edge_rest_kernel, [block] * 4, [pltpu.VMEM((4, rows // 4, atoms), BF16)])(dsrc, picks)
    arrived = [traded(returns[s], swap) for s, swap in enumerate(SWAPS)]
    layer, grad, lent = call(
        after_kernel,
        [
            like((COEFS, pairs, 16, atoms), BF16),
            like((COEFS, channels // 8, 8, atoms), F32),
            like((4, atoms, 2 * atoms), BF16),
        ],
    )(own, cot, src, lists, down, fdown, act, feat, prod, dsrc)
    total = call(
        final_kernel,
        pltpu.HBM((COEFS, channels, atoms), F32),
        [pltpu.VMEM((COEFS, channels, atoms), F32), pltpu.SemaphoreType.DMA((4,))],
        out_spec=HB,
    )(*arrived, lent, grad.reshape(COEFS, channels, atoms))
    return layer.reshape(1, 1, rows, atoms), total.reshape(1, 1, rows, atoms)


def solution(mesh):
    cell = P("gx", "gy", None, None)
    row = P("gx", "gy", None)
    placed = (cell, cell, P(), P(), P(), P(), P(), P(), P(), cell, row, row, cell)
    return jax.shard_map(
        per_device, mesh=mesh, in_specs=placed, out_specs=(cell, cell), check_vma=False
    )
```

```python
import jax
import jax.numpy as jnp
from jax import lax
from jax.experimental import pallas as pl
from jax.experimental.pallas import tpu as pltpu
from jax.sharding import PartitionSpec as P


F32, BF16, I32 = jnp.float32, jnp.bfloat16, jnp.int32
COEFS = 25
DEGREES = 5
edge_norm = 0.35
SWAPS = ((0, None), (1, None), (1, 1), (0, 1), (1, 0), (0, 0), (None, 1), (None, 0))


def parity_along_gx(swap, y, ny):
    if swap[1] is None:
        kind = lax.rem(y, 2)
    else:
        kind = lax.rem(lax.div(lax.rem(y + swap[1], ny), 2), 2)
    return lax.rem(swap[0] + kind, 2)


def step_of(place, parity):
    return jnp.where(lax.rem(place, 2) == parity, 1, -1)


def received_direction(swap):
    x, y = lax.axis_index("gx"), lax.axis_index("gy")
    dx = 0 if swap[0] is None else step_of(x, parity_along_gx(swap, y, lax.axis_size("gy")))
    dy = 0 if swap[1] is None else step_of(y, swap[1])
    place = 3 * (dx + 1) + dy + 1
    return place - jnp.where(place > 4, 1, 0)


def traded(value, swap):
    nx, ny = lax.axis_size("gx"), lax.axis_size("gy")

    def partner(place, size, parity):
        if parity is None:
            return place
        return (place + (1 if place % 2 == parity else -1)) % size

    def parity_x(y):
        if swap[0] is None:
            return None
        kind = y % 2 if swap[1] is None else (y + swap[1]) % ny // 2 % 2
        return (swap[0] + kind) % 2

    pairs = [
        (x * ny + y, partner(x, nx, parity_x(y)) * ny + partner(y, ny, swap[1]))
        for x in range(nx)
        for y in range(ny)
    ]
    return lax.ppermute(value, ("gx", "gy"), pairs)


def iota(shape, axis):
    return lax.broadcasted_iota(I32, shape, axis)


def dot(a, b):
    return jnp.dot(a, b, preferred_element_type=F32)


def dot_nt(a, b):
    return lax.dot_general(a, b, (((1,), (1,)), ((), ())), preferred_element_type=F32)


def split(value):
    high = value.astype(BF16)
    return high, (value - high.astype(F32)).astype(BF16)


def rows_of(value, part):
    rows, width = value.shape
    quarter = rows // COEFS // 4
    return value.reshape(COEFS, 4, quarter, width)[:, part].reshape(COEFS * quarter, width)


def merged(blocks, part):
    width = blocks[0].shape[1] // 4
    lane = iota((1, 4 * width), 1)
    result = blocks[(3 - part) % 4]
    for m in (2, 1, 0):
        result = jnp.where(lane < (m + 1) * width, blocks[(m - part) % 4], result)
    return result


def lent_lists(lists_ref, swaps):
    rows = [lists_ref[pl.ds(7 - received_direction(swap), 1), :] for swap in swaps]
    return [jnp.concatenate([row] * 4, axis=1) for row in rows]


def lent_pick(lists, q):
    row = merged(lists, q)
    return (iota((row.shape[1], row.shape[1]), 0) == row).astype(BF16)


def fetch(sources, targets, sems):
    copies = [pltpu.make_async_copy(a, b, sems.at[n]) for n, (a, b) in enumerate(zip(sources, targets))]
    for copy in copies:
        copy.start()
    return copies


def pack_group(own, lists, outs, scratch):
    for q in range(4):
        scratch[q] = dot(rows_of(own, q), lent_pick(lists, q))
    for k in range(4):
        outs[k][...] = merged([scratch[q] for q in range(4)], k).astype(BF16)


def pack_kernel(own_hbm, lists_hbm, *refs):
    outs, own_ref, lists_ref, scratch, sems = refs[:4], refs[4], refs[5], refs[6], refs[7]
    copies = fetch((lists_hbm, own_hbm), (lists_ref, own_ref), sems)
    copies[0].wait()
    lists = lent_lists(lists_ref, SWAPS[:4])
    copies[1].wait()
    pack_group(own_ref[...], lists, outs, scratch)


def pack_rest_kernel(own_ref, lists_ref, *refs):
    pack_group(own_ref[...], lent_lists(lists_ref, SWAPS[4:]), refs[:4], refs[4])


def equal_bits(shape, axis_shift, other_shift):
    return (
        lax.shift_right_logical(iota(shape, 0), axis_shift)
        == lax.shift_right_logical(iota(shape, 1), other_shift)
    ).astype(BF16)


def up_matrices(parts, s):
    points = parts[0].shape[1]
    rows = equal_bits((2 * points, points), 1, 0)
    cols = equal_bits((COEFS, 8 * COEFS), 0, 3)
    wide = [dot(dot_nt(rows, part).astype(BF16), cols) for part in parts]
    row, col = iota(wide[0].shape, 0), iota(wide[0].shape, 1)
    term = lax.bitwise_and(lax.shift_right_logical(col, 1) - s, 3)
    value = jnp.where(term < 2, wide[0], jnp.where(term == 2, wide[1], 0.0))
    return jnp.where(lax.bitwise_and(row, 1) == lax.bitwise_and(col, 1), value, 0.0).astype(BF16)


def down_matrix(part, padded):
    points = part.shape[1]
    shape = (8 * COEFS, 4 * padded)
    row, col = iota(shape, 0), iota(shape, 1)
    slot = sum((col >= m * padded).astype(I32) for m in (1, 2, 3))
    place = iota((points, 4 * padded), 1)
    place = place - padded * sum((place >= m * padded).astype(I32) for m in (1, 2, 3))
    cols = (lax.shift_right_logical(place, 1) == iota((points, 4 * padded), 0)).astype(BF16)
    wide = dot(dot(equal_bits((8 * COEFS, COEFS), 3, 0), part).astype(BF16), cols)
    inner = lax.bitwise_and(col - padded * slot, 1)
    return jnp.where(lax.bitwise_and(row, 7) == 2 * slot + inner, wide, 0.0).astype(BF16)


def channel_pair(value, p):
    width = value.shape[1]
    shaped = value.reshape(COEFS, value.shape[0] // COEFS // 8, 8, width)
    return jnp.concatenate([shaped[:, 2 * p + h] for h in range(2)], axis=2)


def slotted(high, low):
    shape = (COEFS * 8, high.shape[2])
    slot = lax.bitwise_and(lax.shift_right_logical(iota((shape[0], 1), 0), 1), 3)
    low = pltpu.roll(low, 2, 1).reshape(shape).astype(BF16)
    again = pltpu.roll(high, 4, 1).reshape(shape).astype(BF16)
    high = high.reshape(shape).astype(BF16)
    for s in range(4):
        yield jnp.where(slot == s, high, jnp.where(slot == (s + 1) % 4, low, again))


def filter_rows(columns, harm, filt, q):
    quarter = filt.shape[1] // 4
    scaled = columns.reshape(COEFS, quarter, columns.shape[1]) * harm
    filt[:, q * quarter : (q + 1) * quarter] = scaled.astype(BF16)


def local_kernel(own_ref, *refs):
    given, refs = refs[:11], refs[11:]
    feat_ref, prod_ref, gate_ref, up_ref, down_ref, fdown_ref, part_ref, picks_ref, both_ref = refs[:9]
    turned, kept, refs = refs[9:14], refs[14:23], refs[23:]
    to_ref, from_ref, fup, filt, sems = refs
    copies = fetch(given, (to_ref, from_ref, *kept), sems)
    cot_ref, weights, harm_ref, src_ref, tgt_ref = kept[0], kept[1:6], kept[6], kept[7], kept[8]
    rows, atoms = own_ref.shape
    points = to_ref.shape[1]
    pairs = feat_ref.shape[0]
    padded = feat_ref.shape[1] // 4
    copies[0].wait()
    copies[1].wait()
    to_parts, from_parts = split(to_ref[...]), split(from_ref[...])
    for s in range(4):
        up_ref[s] = up_matrices(to_parts, s)
        fup[s] = up_matrices(from_parts, s)
    for n in range(2):
        down_ref[n] = down_matrix(to_parts[n], padded)
        fdown_ref[n] = down_matrix(from_parts[n], padded)
    for copy in copies[2:]:
        copy.wait()
    own = own_ref[...].astype(F32)
    cot = cot_ref[...].astype(F32)
    for p in range(pairs):
        x = channel_pair(own, p)
        y = channel_pair(cot, p)
        for s, (a, b) in enumerate(zip(slotted(x, jnp.zeros_like(x)), slotted(y, jnp.zeros_like(y)))):
            here = slice(s * padded, s * padded + 2 * points)
            rest = slice(s * padded + 2 * points, (s + 1) * padded)
            feat = dot(up_ref[s], a)
            prod = dot(fup[s], b)
            feat_ref[p, here] = feat
            prod_ref[p, here] = prod
            gate_ref[p, here] = feat * prod
            for ref in (feat_ref, prod_ref):
                ref[p, rest] = jnp.zeros((padded - 2 * points, 2 * atoms), F32)
    src, tgt = src_ref[...], tgt_ref[...]
    edges = src.shape[1]
    ghost = atoms // 4
    target_pick = (iota((atoms, edges), 0) == tgt).astype(BF16)
    both_ref[:atoms] = target_pick
    both_ref[atoms:] = target_pick
    slabs = []
    for swap in SWAPS:
        base = atoms + ghost * received_direction(swap)
        slabs.append((iota((ghost, edges), 0) + base == src).astype(BF16))
    for q in range(4):
        picks_ref[q] = jnp.concatenate(
            [slabs[4 * g + (m - q) % 4] for g in range(2) for m in range(4)], axis=0
        )
    own_pick = (iota((atoms, edges), 0) == src).astype(BF16)
    for q in range(4):
        filter_rows(dot(rows_of(own_ref[...], q), own_pick), harm_ref[...], filt, q)
    part_ref[...] = dot_nt(filt[...].reshape(rows, edges), target_pick)
    turned[0][...] = weights[0][...].T
    for a, b in zip(turned[1:], weights[1:]):
        for n in range(2):
            a[n] = b[n].T


def order_spans(channels):
    spans = []
    offset = DEGREES * channels
    for gap in range(1, DEGREES):
        length = (DEGREES - gap) * channels
        spans.append((offset, offset + length, offset + 2 * length))
        offset += 2 * length
    return spans


def folded(value):
    half = value.shape[1] // 2
    return value[:, :half] + value[:, half:]


def edge_kernel(*refs):
    ghosts, refs = refs[:8], refs[8:]
    weights, turned, refs = refs[:5], refs[5:10], refs[10:]
    picks_ref, both_ref, part_ref, harm_ref, gate_ref, up_ref, down_ref = refs[:7]
    outs, refs = refs[7:11], refs[11:]
    act_ref, dsrc_ref, filt, mixed, agg, dgrid, dagg, packed = refs
    rows, atoms = part_ref.shape
    channels = rows // COEFS
    edges = both_ref.shape[1]
    pairs = act_ref.shape[0]
    padded = act_ref.shape[1] // 4
    used = up_ref.shape[1]
    blocks = [ghosts[s][...] for s in range(8)]
    for q in range(4):
        taken = jnp.concatenate([merged(blocks[4 * g : 4 * g + 4], q) for g in range(2)], axis=1)
        filter_rows(dot(taken, picks_ref[q]), harm_ref[...], filt, q)
    summed = part_ref[...] + dot_nt(filt[...].reshape(rows, edges), both_ref[:atoms])
    high, low = split(summed)
    mixed[:, :atoms] = high
    mixed[:, atoms:] = low
    zero_rows = DEGREES * channels
    half = 0.5 * edge_norm
    agg[:zero_rows] = folded(dot(weights[0][...], mixed[:zero_rows])) * half
    for w, (begin, mid, end) in zip(weights[1:], order_spans(channels)):
        plus, minus = mixed[begin:mid], mixed[mid:end]
        agg[begin:mid] = folded(dot(w[0], plus) - dot(w[1], minus)) * half
        agg[mid:end] = folded(dot(w[1], plus) + dot(w[0], minus)) * half
    empty = jnp.zeros((padded - used, 2 * atoms), F32)
    for s in range(4):
        rest = slice(s * padded + used, (s + 1) * padded)
        dgrid[rest] = empty.astype(BF16)
    for p in range(pairs):
        x = channel_pair(agg[...], p)
        high = x.astype(BF16).astype(F32)
        for s, side in enumerate(slotted(high, x - high)):
            here = slice(s * padded, s * padded + used)
            h = dot(up_ref[s], side)
            t = jnp.tanh(h)
            u = 1.0 + t
            act = h * u
            act_ref[p, here] = act
            act_ref[p, s * padded + used : (s + 1) * padded] = empty
            dgrid[here] = (gate_ref[p, here] * (u + act * (1.0 - t))).astype(BF16)
        down = dot(down_ref[0], dgrid[...]) * half
        for n in range(2):
            dagg[:, 2 * p + n] = down[:, n * atoms : (n + 1) * atoms].reshape(COEFS, 8, atoms)
    back = dagg[...].reshape(rows, atoms).astype(BF16)

    def keep(begin, end, value):
        high, low = split(value)
        mixed[begin:end, :atoms] = high
        mixed[begin:end, atoms:] = low

    keep(0, zero_rows, dot(turned[0][...], back[:zero_rows]))
    for w, (begin, mid, end) in zip(turned[1:], order_spans(channels)):
        side = jnp.concatenate([back[begin:mid], back[mid:end]], axis=1)
        first, second = dot(w[0], side), dot(w[1], side)
        keep(begin, mid, first[:, :atoms] + second[:, atoms:])
        keep(mid, end, first[:, atoms:] - second[:, :atoms])
    for q in range(4):
        grads = dot(rows_of(mixed[...], q), both_ref[...])
        shaped = grads.reshape(COEFS, grads.shape[0] // COEFS, edges) * harm_ref[...]
        scaled = shaped.reshape(grads.shape).astype(BF16)
        dsrc_ref[q] = scaled
    return_group(dsrc_ref, picks_ref, outs, packed, 0)


def return_group(dsrc_ref, picks_ref, outs, packed, g):
    half = picks_ref.shape[1] // 2
    for q in range(4):
        packed[q] = dot_nt(dsrc_ref[q], picks_ref[q, g * half : (g + 1) * half]).astype(BF16)
    for k in range(4):
        outs[k][...] = merged([packed[q] for q in range(4)], k)


def edge_rest_kernel(dsrc_ref, picks_ref, *refs):
    return_group(dsrc_ref, picks_ref, refs[:4], refs[4], 1)


def after_kernel(*refs):
    own_ref, cot_ref, src_ref, lists_ref, down_ref, fdown_ref = refs[:6]
    act_ref, feat_ref, prod_ref, dsrc_ref, out_ref, grad_ref, lent_ref = refs[6:]
    rows, atoms = own_ref.shape
    channels = rows // COEFS
    edges = src_ref.shape[1]
    own_pick = (iota((atoms, edges), 0) == src_ref[...]).astype(BF16)
    own = own_ref[...].astype(F32).reshape(COEFS, channels // 8, 8, atoms)
    cot = cot_ref[...].astype(F32).reshape(COEFS, channels // 8, 8, atoms)

    for g in range(2):
        lists = lent_lists(lists_ref, SWAPS[4 * g : 4 * g + 4])
        for q in range(4):
            lent_ref[q, :, g * atoms : (g + 1) * atoms] = lent_pick(lists, q)

    def down(parts, value):
        high, low = split(value)
        return dot(parts[0], high) + dot(parts[0], low) + dot(parts[1], high)

    for p in range(channels // 16):
        act = act_ref[p]
        update = down(fdown_ref, act * feat_ref[p])
        grad = down(down_ref, prod_ref[p] * act)
        here = dot_nt(dsrc_ref[p], own_pick).reshape(COEFS, 2, 8, atoms)
        outs = []
        for h in range(2):
            lanes = slice(h * atoms, (h + 1) * atoms)
            outs.append(own[:, 2 * p + h] + update[:, lanes].reshape(COEFS, 8, atoms))
            grad_ref[:, 2 * p + h] = (
                cot[:, 2 * p + h] + grad[:, lanes].reshape(COEFS, 8, atoms) + here[:, h]
            )
        out_ref[:, p] = jnp.concatenate(outs, axis=1).astype(BF16)


def final_kernel(*refs):
    blocks = [r[...] for r in refs[:8]]
    lent_ref, grad_ref, out_hbm, total, sems = refs[8:]
    atoms = grad_ref.shape[2]
    copies = []
    for q in range(4):
        taken = jnp.concatenate([merged(blocks[4 * g : 4 * g + 4], q) for g in range(2)], axis=1)
        added = dot_nt(taken, lent_ref[q])
        quarter = added.shape[0] // COEFS
        here = slice(q * quarter, (q + 1) * quarter)
        total[:, here] = grad_ref[:, here] + added.reshape(COEFS, quarter, atoms)
        copies.append(pltpu.make_async_copy(total.at[:, here], out_hbm.at[:, here], sems.at[q]))
        copies[-1].start()
    for copy in copies:
        copy.wait()


VM = pl.BlockSpec(memory_space=pltpu.VMEM)
HB = pl.BlockSpec(memory_space=pltpu.HBM)


def call(kernel, outs, scratch=(), far=(), out_spec=VM):
    def run(*args):
        args = [pltpu.with_memory_space_constraint(x, pltpu.HBM) if n in far else x for n, x in enumerate(args)]
        return pl.pallas_call(
            kernel,
            out_shape=outs,
            in_specs=[HB if n in far else VM for n in range(len(args))],
            out_specs=jax.tree.map(lambda _: out_spec, outs),
            scratch_shapes=list(scratch),
            compiler_params=pltpu.CompilerParams(vmem_limit_bytes=20 * 1024 * 1024),
        )(*args)

    return run


def per_device(
    features,
    cotangent,
    w_order0,
    w_order1,
    w_order2,
    w_order3,
    w_order4,
    to_grid,
    from_grid,
    edge_harmonics,
    edge_source,
    edge_target,
    send_list,
):
    rows, atoms = features.shape[2:]
    channels = rows // COEFS
    edges = edge_source.shape[2]
    points = to_grid.shape[0]
    padded = -(-2 * points // 16) * 16
    pairs = channels // 16
    like = jax.ShapeDtypeStruct
    same = lambda x: like(x.shape, x.dtype)
    block = like((rows // 4, atoms), BF16)
    grid = like((pairs, 4 * padded, 2 * atoms), F32)
    *packed, own, lists = call(
        pack_kernel,
        [block] * 4 + [like((rows, atoms), BF16), like(send_list.shape[2:], I32)],
        [pltpu.VMEM((4, rows // 4, atoms), F32), pltpu.SemaphoreType.DMA((2,))],
        (0, 1),
    )(features[0, 0], send_list[0, 0])
    packed += call(pack_rest_kernel, [block] * 4, [pltpu.VMEM((4, rows // 4, atoms), F32)])(own, lists)
    ghosts = [traded(packed[s], swap) for s, swap in enumerate(SWAPS)]
    weights = (w_order0, w_order1, w_order2, w_order3, w_order4)
    kept = (
        cotangent[0, 0],
        *weights,
        edge_harmonics[0, 0][:, None, :],
        edge_source[0],
        edge_target[0],
    )
    given = (to_grid.T, from_grid, *kept)
    downs = like((2, 8 * COEFS, 4 * padded), BF16)
    feat, prod, gate, up, down, fdown, part, picks, both, *near = call(
        local_kernel,
        [
            grid,
            grid,
            grid,
            like((4, 2 * points, 8 * COEFS), BF16),
            downs,
            downs,
            like((rows, atoms), F32),
            like((4, 2 * atoms, edges), BF16),
            like((2 * atoms, edges), BF16),
            *map(same, weights),
            *map(same, kept),
        ],
        [
            pltpu.VMEM((COEFS, points), F32),
            pltpu.VMEM((COEFS, points), F32),
            pltpu.VMEM((4, 2 * points, 8 * COEFS), BF16),
            pltpu.VMEM((COEFS, channels, edges), BF16),
            pltpu.SemaphoreType.DMA((len(given),)),
        ],
        range(1, 1 + len(given)),
    )(own, *given)
    turned, (cot, *direct, harm, src, tgt) = near[:5], near[5:]
    *returns, act, dsrc = call(
        edge_kernel,
        [block] * 4 + [grid, like((4, rows // 4, edges), BF16)],
        [
            pltpu.VMEM((COEFS, channels, edges), BF16),
            pltpu.VMEM((rows, 2 * atoms), BF16),
            pltpu.VMEM((rows, atoms), F32),
            pltpu.VMEM((4 * padded, 2 * atoms), BF16),
            pltpu.VMEM((COEFS, channels // 8, 8, atoms), F32),
            pltpu.VMEM((4, rows // 4, atoms), BF16),
        ],
    )(*ghosts, *direct, *turned, picks, both, part, harm, gate, up, down)
    returns += call(edge_rest_kernel, [block] * 4, [pltpu.VMEM((4, rows // 4, atoms), BF16)])(dsrc, picks)
    arrived = [traded(returns[s], swap) for s, swap in enumerate(SWAPS)]
    layer, grad, lent = call(
        after_kernel,
        [
            like((COEFS, pairs, 16, atoms), BF16),
            like((COEFS, channels // 8, 8, atoms), F32),
            like((4, atoms, 2 * atoms), BF16),
        ],
    )(own, cot, src, lists, down, fdown, act, feat, prod, dsrc)
    total = call(
        final_kernel,
        pltpu.HBM((COEFS, channels, atoms), F32),
        [pltpu.VMEM((COEFS, channels, atoms), F32), pltpu.SemaphoreType.DMA((4,))],
        out_spec=HB,
    )(*arrived, lent, grad.reshape(COEFS, channels, atoms))
    return layer.reshape(1, 1, rows, atoms), total.reshape(1, 1, rows, atoms)


def solution(mesh):
    cell = P("gx", "gy", None, None)
    row = P("gx", "gy", None)
    placed = (cell, cell, P(), P(), P(), P(), P(), P(), P(), cell, row, row, cell)
    return jax.shard_map(
        per_device, mesh=mesh, in_specs=placed, out_specs=(cell, cell), check_vma=False
    )
```

```python
import jax
import jax.numpy as jnp
from jax import lax
from jax.experimental import pallas as pl
from jax.experimental.pallas import tpu as pltpu
from jax.sharding import PartitionSpec as P


F32, BF16, I32 = jnp.float32, jnp.bfloat16, jnp.int32
COEFS = 25
DEGREES = 5
edge_norm = 0.35
SWAPS = ((0, None), (1, None), (1, 1), (0, 1), (1, 0), (0, 0), (None, 1), (None, 0))


def parity_along_gx(swap, y, ny):
    if swap[1] is None:
        kind = lax.rem(y, 2)
    else:
        kind = lax.rem(lax.div(lax.rem(y + swap[1], ny), 2), 2)
    return lax.rem(swap[0] + kind, 2)


def step_of(place, parity):
    return jnp.where(lax.rem(place, 2) == parity, 1, -1)


def received_direction(swap):
    x, y = lax.axis_index("gx"), lax.axis_index("gy")
    dx = 0 if swap[0] is None else step_of(x, parity_along_gx(swap, y, lax.axis_size("gy")))
    dy = 0 if swap[1] is None else step_of(y, swap[1])
    place = 3 * (dx + 1) + dy + 1
    return place - jnp.where(place > 4, 1, 0)


def traded(value, swap):
    nx, ny = lax.axis_size("gx"), lax.axis_size("gy")

    def partner(place, size, parity):
        if parity is None:
            return place
        return (place + (1 if place % 2 == parity else -1)) % size

    def parity_x(y):
        if swap[0] is None:
            return None
        kind = y % 2 if swap[1] is None else (y + swap[1]) % ny // 2 % 2
        return (swap[0] + kind) % 2

    pairs = [
        (x * ny + y, partner(x, nx, parity_x(y)) * ny + partner(y, ny, swap[1]))
        for x in range(nx)
        for y in range(ny)
    ]
    return lax.ppermute(value, ("gx", "gy"), pairs)


def iota(shape, axis):
    return lax.broadcasted_iota(I32, shape, axis)


def dot(a, b):
    return jnp.dot(a, b, preferred_element_type=F32)


def dot_nt(a, b):
    return lax.dot_general(a, b, (((1,), (1,)), ((), ())), preferred_element_type=F32)


def split(value):
    high = value.astype(BF16)
    return high, (value - high.astype(F32)).astype(BF16)


def rows_of(value, part):
    rows, width = value.shape
    quarter = rows // COEFS // 4
    return value.reshape(COEFS, 4, quarter, width)[:, part].reshape(COEFS * quarter, width)


def merged(blocks, part):
    width = blocks[0].shape[1] // 4
    lane = iota((1, 4 * width), 1)
    result = blocks[(3 - part) % 4]
    for m in (2, 1, 0):
        result = jnp.where(lane < (m + 1) * width, blocks[(m - part) % 4], result)
    return result


def lent_lists(lists_ref, swaps):
    rows = [lists_ref[pl.ds(7 - received_direction(swap), 1), :] for swap in swaps]
    return [jnp.concatenate([row] * 4, axis=1) for row in rows]


def lent_pick(lists, q):
    row = merged(lists, q)
    return (iota((row.shape[1], row.shape[1]), 0) == row).astype(BF16)


def fetch(sources, targets, sems):
    copies = [pltpu.make_async_copy(a, b, sems.at[n]) for n, (a, b) in enumerate(zip(sources, targets))]
    for copy in copies:
        copy.start()
    return copies


def pack_group(own, lists, outs, scratch):
    for q in range(4):
        scratch[q] = dot(rows_of(own, q), lent_pick(lists, q))
    for k in range(4):
        outs[k][...] = merged([scratch[q] for q in range(4)], k).astype(BF16)


def pack_kernel(own_hbm, lists_hbm, *refs):
    outs, own_ref, lists_ref, scratch, sems = refs[:4], refs[4], refs[5], refs[6], refs[7]
    copies = fetch((lists_hbm, own_hbm), (lists_ref, own_ref), sems)
    copies[0].wait()
    lists = lent_lists(lists_ref, SWAPS[:4])
    copies[1].wait()
    pack_group(own_ref[...], lists, outs, scratch)


def pack_rest_kernel(own_ref, lists_ref, *refs):
    pack_group(own_ref[...], lent_lists(lists_ref, SWAPS[4:]), refs[:4], refs[4])


def equal_bits(shape, axis_shift, other_shift):
    return (
        lax.shift_right_logical(iota(shape, 0), axis_shift)
        == lax.shift_right_logical(iota(shape, 1), other_shift)
    ).astype(BF16)


def up_matrices(parts, s):
    points = parts[0].shape[1]
    rows = equal_bits((2 * points, points), 1, 0)
    cols = equal_bits((COEFS, 8 * COEFS), 0, 3)
    wide = [dot(dot_nt(rows, part).astype(BF16), cols) for part in parts]
    row, col = iota(wide[0].shape, 0), iota(wide[0].shape, 1)
    term = lax.bitwise_and(lax.shift_right_logical(col, 1) - s, 3)
    value = jnp.where(term < 2, wide[0], jnp.where(term == 2, wide[1], 0.0))
    return jnp.where(lax.bitwise_and(row, 1) == lax.bitwise_and(col, 1), value, 0.0).astype(BF16)


def down_matrix(part, padded):
    points = part.shape[1]
    shape = (8 * COEFS, 4 * padded)
    row, col = iota(shape, 0), iota(shape, 1)
    slot = sum((col >= m * padded).astype(I32) for m in (1, 2, 3))
    place = iota((points, 4 * padded), 1)
    place = place - padded * sum((place >= m * padded).astype(I32) for m in (1, 2, 3))
    cols = (lax.shift_right_logical(place, 1) == iota((points, 4 * padded), 0)).astype(BF16)
    wide = dot(dot(equal_bits((8 * COEFS, COEFS), 3, 0), part).astype(BF16), cols)
    inner = lax.bitwise_and(col - padded * slot, 1)
    return jnp.where(lax.bitwise_and(row, 7) == 2 * slot + inner, wide, 0.0).astype(BF16)


def channel_pair(value, p):
    width = value.shape[1]
    shaped = value.reshape(COEFS, value.shape[0] // COEFS // 8, 8, width)
    return jnp.concatenate([shaped[:, 2 * p + h] for h in range(2)], axis=2)


def slotted(high, low):
    shape = (COEFS * 8, high.shape[2])
    slot = lax.bitwise_and(lax.shift_right_logical(iota((shape[0], 1), 0), 1), 3)
    low = pltpu.roll(low, 2, 1).reshape(shape).astype(BF16)
    again = pltpu.roll(high, 4, 1).reshape(shape).astype(BF16)
    high = high.reshape(shape).astype(BF16)
    for s in range(4):
        yield jnp.where(slot == s, high, jnp.where(slot == (s + 1) % 4, low, again))


def filter_rows(columns, harm, filt, q):
    quarter = filt.shape[1] // 4
    scaled = columns.reshape(COEFS, quarter, columns.shape[1]) * harm
    filt[:, q * quarter : (q + 1) * quarter] = scaled.astype(BF16)


def local_kernel(own_ref, *refs):
    given, refs = refs[:11], refs[11:]
    feat_ref, prod_ref, gate_ref, up_ref, down_ref, from_ref, part_ref, picks_ref, both_ref = refs[:9]
    turned, kept, refs = refs[9:14], refs[14:23], refs[23:]
    to_ref, fup, filt, sems = refs
    copies = fetch(given, (to_ref, from_ref, *kept), sems)
    cot_ref, weights, harm_ref, src_ref, tgt_ref = kept[0], kept[1:6], kept[6], kept[7], kept[8]
    rows, atoms = own_ref.shape
    points = to_ref.shape[1]
    pairs = feat_ref.shape[0]
    padded = feat_ref.shape[1] // 4
    copies[0].wait()
    copies[1].wait()
    to_parts, from_parts = split(to_ref[...]), split(from_ref[...])
    for s in range(4):
        up_ref[s] = up_matrices(to_parts, s)
        fup[s] = up_matrices(from_parts, s)
    for n in range(2):
        down_ref[n] = down_matrix(to_parts[n], padded)
    for copy in copies[2:]:
        copy.wait()
    own = own_ref[...].astype(F32)
    cot = cot_ref[...].astype(F32)
    for p in range(pairs):
        x = channel_pair(own, p)
        y = channel_pair(cot, p)
        for s, (a, b) in enumerate(zip(slotted(x, jnp.zeros_like(x)), slotted(y, jnp.zeros_like(y)))):
            here = slice(s * padded, s * padded + 2 * points)
            rest = slice(s * padded + 2 * points, (s + 1) * padded)
            feat = dot(up_ref[s], a)
            prod = dot(fup[s], b)
            feat_ref[p, here] = feat
            prod_ref[p, here] = prod
            gate_ref[p, here] = feat * prod
            for ref in (feat_ref, prod_ref):
                ref[p, rest] = jnp.zeros((padded - 2 * points, 2 * atoms), F32)
    src, tgt = src_ref[...], tgt_ref[...]
    edges = src.shape[1]
    ghost = atoms // 4
    target_pick = (iota((atoms, edges), 0) == tgt).astype(BF16)
    both_ref[:atoms] = target_pick
    both_ref[atoms:] = target_pick
    slabs = []
    for swap in SWAPS:
        base = atoms + ghost * received_direction(swap)
        slabs.append((iota((ghost, edges), 0) + base == src).astype(BF16))
    for q in range(4):
        picks_ref[q] = jnp.concatenate(
            [slabs[4 * g + (m - q) % 4] for g in range(2) for m in range(4)], axis=0
        )
    own_pick = (iota((atoms, edges), 0) == src).astype(BF16)
    for q in range(4):
        filter_rows(dot(rows_of(own_ref[...], q), own_pick), harm_ref[...], filt, q)
    part_ref[...] = dot_nt(filt[...].reshape(rows, edges), target_pick)
    turned[0][...] = weights[0][...].T
    for a, b in zip(turned[1:], weights[1:]):
        for n in range(2):
            a[n] = b[n].T


def order_spans(channels):
    spans = []
    offset = DEGREES * channels
    for gap in range(1, DEGREES):
        length = (DEGREES - gap) * channels
        spans.append((offset, offset + length, offset + 2 * length))
        offset += 2 * length
    return spans


def folded(value):
    half = value.shape[1] // 2
    return value[:, :half] + value[:, half:]


def edge_kernel(*refs):
    ghosts, refs = refs[:8], refs[8:]
    weights, turned, refs = refs[:5], refs[5:10], refs[10:]
    picks_ref, both_ref, part_ref, harm_ref, gate_ref, up_ref, down_ref = refs[:7]
    outs, refs = refs[7:11], refs[11:]
    act_ref, dsrc_ref, filt, mixed, agg, dgrid, dagg, packed = refs
    rows, atoms = part_ref.shape
    channels = rows // COEFS
    edges = both_ref.shape[1]
    pairs = act_ref.shape[0]
    padded = act_ref.shape[1] // 4
    used = up_ref.shape[1]
    blocks = [ghosts[s][...] for s in range(8)]
    for q in range(4):
        taken = jnp.concatenate([merged(blocks[4 * g : 4 * g + 4], q) for g in range(2)], axis=1)
        filter_rows(dot(taken, picks_ref[q]), harm_ref[...], filt, q)
    summed = part_ref[...] + dot_nt(filt[...].reshape(rows, edges), both_ref[:atoms])
    high, low = split(summed)
    mixed[:, :atoms] = high
    mixed[:, atoms:] = low
    zero_rows = DEGREES * channels
    half = 0.5 * edge_norm
    agg[:zero_rows] = folded(dot(weights[0][...], mixed[:zero_rows])) * half
    for w, (begin, mid, end) in zip(weights[1:], order_spans(channels)):
        plus, minus = mixed[begin:mid], mixed[mid:end]
        agg[begin:mid] = folded(dot(w[0], plus) - dot(w[1], minus)) * half
        agg[mid:end] = folded(dot(w[1], plus) + dot(w[0], minus)) * half
    empty = jnp.zeros((padded - used, 2 * atoms), F32)
    for s in range(4):
        rest = slice(s * padded + used, (s + 1) * padded)
        dgrid[rest] = empty.astype(BF16)
    for p in range(pairs):
        x = channel_pair(agg[...], p)
        high = x.astype(BF16).astype(F32)
        for s, side in enumerate(slotted(high, x - high)):
            here = slice(s * padded, s * padded + used)
            h = dot(up_ref[s], side)
            t = jnp.tanh(h)
            u = 1.0 + t
            act = h * u
            act_ref[p, here] = act
            act_ref[p, s * padded + used : (s + 1) * padded] = empty
            dgrid[here] = (gate_ref[p, here] * (u + act * (1.0 - t))).astype(BF16)
        down = dot(down_ref[0], dgrid[...]) * half
        for n in range(2):
            dagg[:, 2 * p + n] = down[:, n * atoms : (n + 1) * atoms].reshape(COEFS, 8, atoms)
    back = dagg[...].reshape(rows, atoms).astype(BF16)

    def keep(begin, end, value):
        high, low = split(value)
        mixed[begin:end, :atoms] = high
        mixed[begin:end, atoms:] = low

    keep(0, zero_rows, dot(turned[0][...], back[:zero_rows]))
    for w, (begin, mid, end) in zip(turned[1:], order_spans(channels)):
        side = jnp.concatenate([back[begin:mid], back[mid:end]], axis=1)
        first, second = dot(w[0], side), dot(w[1], side)
        keep(begin, mid, first[:, :atoms] + second[:, atoms:])
        keep(mid, end, first[:, atoms:] - second[:, :atoms])
    for q in range(4):
        grads = dot(rows_of(mixed[...], q), both_ref[...])
        shaped = grads.reshape(COEFS, grads.shape[0] // COEFS, edges) * harm_ref[...]
        scaled = shaped.reshape(grads.shape).astype(BF16)
        dsrc_ref[q] = scaled
    return_group(dsrc_ref, picks_ref, outs, packed, 0)


def return_group(dsrc_ref, picks_ref, outs, packed, g):
    half = picks_ref.shape[1] // 2
    for q in range(4):
        packed[q] = dot_nt(dsrc_ref[q], picks_ref[q, g * half : (g + 1) * half]).astype(BF16)
    for k in range(4):
        outs[k][...] = merged([packed[q] for q in range(4)], k)


def edge_rest_kernel(dsrc_ref, picks_ref, *refs):
    return_group(dsrc_ref, picks_ref, refs[:4], refs[4], 1)


def after_kernel(*refs):
    own_ref, cot_ref, src_ref, lists_ref, down_ref, from_ref = refs[:6]
    act_ref, feat_ref, prod_ref, dsrc_ref, out_ref, grad_ref, lent_ref, fdown_ref = refs[6:]
    rows, atoms = own_ref.shape
    channels = rows // COEFS
    edges = src_ref.shape[1]
    own_pick = (iota((atoms, edges), 0) == src_ref[...]).astype(BF16)
    own = own_ref[...].astype(F32).reshape(COEFS, channels // 8, 8, atoms)
    cot = cot_ref[...].astype(F32).reshape(COEFS, channels // 8, 8, atoms)

    for g in range(2):
        lists = lent_lists(lists_ref, SWAPS[4 * g : 4 * g + 4])
        for q in range(4):
            lent_ref[q, :, g * atoms : (g + 1) * atoms] = lent_pick(lists, q)

    for n, part in enumerate(split(from_ref[...])):
        fdown_ref[n] = down_matrix(part, fdown_ref.shape[2] // 4)

    def down(parts, value):
        high, low = split(value)
        return dot(parts[0], high) + dot(parts[0], low) + dot(parts[1], high)

    for p in range(channels // 16):
        act = act_ref[p]
        update = down(fdown_ref, act * feat_ref[p])
        grad = down(down_ref, prod_ref[p] * act)
        here = dot_nt(dsrc_ref[p], own_pick).reshape(COEFS, 2, 8, atoms)
        outs = []
        for h in range(2):
            lanes = slice(h * atoms, (h + 1) * atoms)
            outs.append(own[:, 2 * p + h] + update[:, lanes].reshape(COEFS, 8, atoms))
            grad_ref[:, 2 * p + h] = (
                cot[:, 2 * p + h] + grad[:, lanes].reshape(COEFS, 8, atoms) + here[:, h]
            )
        out_ref[:, p] = jnp.concatenate(outs, axis=1).astype(BF16)


def final_kernel(*refs):
    blocks = [r[...] for r in refs[:8]]
    lent_ref, grad_ref, out_hbm, total, sems = refs[8:]
    atoms = grad_ref.shape[2]
    copies = []
    for q in range(4):
        taken = jnp.concatenate([merged(blocks[4 * g : 4 * g + 4], q) for g in range(2)], axis=1)
        added = dot_nt(taken, lent_ref[q])
        quarter = added.shape[0] // COEFS
        here = slice(q * quarter, (q + 1) * quarter)
        total[:, here] = grad_ref[:, here] + added.reshape(COEFS, quarter, atoms)
        copies.append(pltpu.make_async_copy(total.at[:, here], out_hbm.at[:, here], sems.at[q]))
        copies[-1].start()
    for copy in copies:
        copy.wait()


VM = pl.BlockSpec(memory_space=pltpu.VMEM)
HB = pl.BlockSpec(memory_space=pltpu.HBM)


def call(kernel, outs, scratch=(), far=(), out_spec=VM):
    def run(*args):
        args = [pltpu.with_memory_space_constraint(x, pltpu.HBM) if n in far else x for n, x in enumerate(args)]
        return pl.pallas_call(
            kernel,
            out_shape=outs,
            in_specs=[HB if n in far else VM for n in range(len(args))],
            out_specs=jax.tree.map(lambda _: out_spec, outs),
            scratch_shapes=list(scratch),
            compiler_params=pltpu.CompilerParams(vmem_limit_bytes=20 * 1024 * 1024),
        )(*args)

    return run


def per_device(
    features,
    cotangent,
    w_order0,
    w_order1,
    w_order2,
    w_order3,
    w_order4,
    to_grid,
    from_grid,
    edge_harmonics,
    edge_source,
    edge_target,
    send_list,
):
    rows, atoms = features.shape[2:]
    channels = rows // COEFS
    edges = edge_source.shape[2]
    points = to_grid.shape[0]
    padded = -(-2 * points // 16) * 16
    pairs = channels // 16
    like = jax.ShapeDtypeStruct
    same = lambda x: like(x.shape, x.dtype)
    block = like((rows // 4, atoms), BF16)
    grid = like((pairs, 4 * padded, 2 * atoms), F32)
    *packed, own, lists = call(
        pack_kernel,
        [block] * 4 + [like((rows, atoms), BF16), like(send_list.shape[2:], I32)],
        [pltpu.VMEM((4, rows // 4, atoms), F32), pltpu.SemaphoreType.DMA((2,))],
        (0, 1),
    )(features[0, 0], send_list[0, 0])
    packed += call(pack_rest_kernel, [block] * 4, [pltpu.VMEM((4, rows // 4, atoms), F32)])(own, lists)
    ghosts = [traded(packed[s], swap) for s, swap in enumerate(SWAPS)]
    weights = (w_order0, w_order1, w_order2, w_order3, w_order4)
    kept = (
        cotangent[0, 0],
        *weights,
        edge_harmonics[0, 0][:, None, :],
        edge_source[0],
        edge_target[0],
    )
    given = (to_grid.T, from_grid, *kept)
    downs = like((2, 8 * COEFS, 4 * padded), BF16)
    feat, prod, gate, up, down, from_near, part, picks, both, *near = call(
        local_kernel,
        [
            grid,
            grid,
            grid,
            like((4, 2 * points, 8 * COEFS), BF16),
            downs,
            same(from_grid),
            like((rows, atoms), F32),
            like((4, 2 * atoms, edges), BF16),
            like((2 * atoms, edges), BF16),
            *map(same, weights),
            *map(same, kept),
        ],
        [
            pltpu.VMEM((COEFS, points), F32),
            pltpu.VMEM((4, 2 * points, 8 * COEFS), BF16),
            pltpu.VMEM((COEFS, channels, edges), BF16),
            pltpu.SemaphoreType.DMA((len(given),)),
        ],
        range(1, 1 + len(given)),
    )(own, *given)
    turned, (cot, *direct, harm, src, tgt) = near[:5], near[5:]
    *returns, act, dsrc = call(
        edge_kernel,
        [block] * 4 + [grid, like((4, rows // 4, edges), BF16)],
        [
            pltpu.VMEM((COEFS, channels, edges), BF16),
            pltpu.VMEM((rows, 2 * atoms), BF16),
            pltpu.VMEM((rows, atoms), F32),
            pltpu.VMEM((4 * padded, 2 * atoms), BF16),
            pltpu.VMEM((COEFS, channels // 8, 8, atoms), F32),
            pltpu.VMEM((4, rows // 4, atoms), BF16),
        ],
    )(*ghosts, *direct, *turned, picks, both, part, harm, gate, up, down)
    returns += call(edge_rest_kernel, [block] * 4, [pltpu.VMEM((4, rows // 4, atoms), BF16)])(dsrc, picks)
    arrived = [traded(returns[s], swap) for s, swap in enumerate(SWAPS)]
    layer, grad, lent = call(
        after_kernel,
        [
            like((COEFS, pairs, 16, atoms), BF16),
            like((COEFS, channels // 8, 8, atoms), F32),
            like((4, atoms, 2 * atoms), BF16),
        ],
        [pltpu.VMEM(downs.shape, BF16)],
    )(own, cot, src, lists, down, from_near, act, feat, prod, dsrc)
    total = call(
        final_kernel,
        pltpu.HBM((COEFS, channels, atoms), F32),
        [pltpu.VMEM((COEFS, channels, atoms), F32), pltpu.SemaphoreType.DMA((4,))],
        out_spec=HB,
    )(*arrived, lent, grad.reshape(COEFS, channels, atoms))
    return layer.reshape(1, 1, rows, atoms), total.reshape(1, 1, rows, atoms)


def solution(mesh):
    cell = P("gx", "gy", None, None)
    row = P("gx", "gy", None)
    placed = (cell, cell, P(), P(), P(), P(), P(), P(), P(), cell, row, row, cell)
    return jax.shard_map(
        per_device, mesh=mesh, in_specs=placed, out_specs=(cell, cell), check_vma=False
    )
```
